256 devices in a mesh: start: 2 (over core), pencil: 128 (over z, x, y).
Axes of the slice: x: 4, y: 4, z: 8, core: 2. Of those that a mesh axis runs over, the one named last changes fastest.
Arguments:
- template: bfloat16 [512, 64, 512], P('pencil', 'start'), parts along dimension 1, may hold values from -3.5 to 3.5
- reference_image: bfloat16 [512, 64, 512], P('pencil', 'start'), parts along dimension 1, may hold values from -3.5 to 3.5
- velocity: float32 [6, 512, 32, 512], P('start', 'pencil'), parts along dimension 0, may hold values from -4 to 4
- dep_owner: int32 [4, 32768], P('start', 'pencil'), parts along dimension 0, may hold values from 0 to 127, as said below
- dep_offset: int32 [4, 32768], P('start', 'pencil'), parts along dimension 0, may hold values from 0 to 255, as said below
- dep_weight: int32 [4, 32768], P('start', 'pencil'), parts along dimension 0, may hold values from 0 to 15
Outputs:
- warped: bfloat16 [512, 64, 512], P('pencil', 'start'), parts along dimension 1
- gradient: float32 [6, 512, 32, 512], P('start', 'pencil'), parts along dimension 0
The draws below stay inside these ranges and needn't reach their ends.
There are 2 independent parts, one for each index of `start`. The reference program is written for one: setup_inputs(seed, part) draws one part's arguments, and reference() takes and returns one part's arrays. A program takes and returns all parts, laid end to end along the dimension named above; each array names one. Nothing has to cross between parts.
Inputs may be any that keep to these rules, and one draw needn't show every extreme that they name: Device d holds blocks d * 256 to (d + 1) * 256 - 1. For a block of device d, dep_owner is (d + m) mod 128 with m one of -2, -1, 0, 1, so that its stencil rows lie on devices d - 2 to d + 2 (modulo 128). dep_offset = r P + g with P as in the reference program, g the block's own in-row number and r < 4; r >= 1 where m = -2.
All inputs are finite; a program needn't handle non-finite values.
Results may differ from the reference program's by a relative error of at most 0.012.
Values may be sent and summed in bfloat16 or wider, within the bound.
No kernel may reach another device: no remote copies, remote signals or barrier semaphores. Data moves between devices by JAX's collectives and lax.ppermute only.
A program may use at most 192 MiB of HBM per device.

```python
import math
import jax
import jax.numpy as jnp
from jax import lax

ROWS = 4
NZ = 32
NY = 512
ZB = 2
SEG = 128
Q = 16
NX = 512
BLK_DEV = 256
N_PENCIL = 128


def rough_field(key):
    grid_field = jax.random.normal(key, (NX, NZ, NY), jnp.float32)
    return jnp.clip(grid_field, -3.5, 3.5).astype(jnp.bfloat16)


def draw_template(key, part):
    return rough_field(jax.random.fold_in(key, 3))


def draw_reference_image(key, part):
    return rough_field(jax.random.fold_in(key, 5))


def departures(key):
    owners = []
    offsets = []
    levels = []
    per_row = NZ // ZB * (NY // SEG)
    device_ids = jnp.arange(N_PENCIL, dtype=jnp.int32)[:, None]
    own_place = (jnp.arange(BLK_DEV, dtype=jnp.int32) % per_row)[None, :]
    for section_index in range(2):
        section_key = jax.random.fold_in(key, 17 + section_index)
        device_keys = jax.random.split(jax.random.fold_in(section_key, 2), N_PENCIL)
        block_order = jax.vmap(lambda device_key: jax.random.permutation(device_key, BLK_DEV))(device_keys)
        move = (block_order % 4).astype(jnp.int32) - 2
        block_owner = (device_ids + move + N_PENCIL) % N_PENCIL
        row_any = jax.random.randint(jax.random.fold_in(section_key, 4), (N_PENCIL, BLK_DEV), 0, ROWS)
        row_spill = jax.random.randint(jax.random.fold_in(section_key, 5), (N_PENCIL, BLK_DEV), 1, ROWS)
        start_row = jnp.where(move == -2, row_spill, row_any)
        offset = start_row * per_row + own_place
        weight_level = jax.random.randint(jax.random.fold_in(section_key, 8), (N_PENCIL, BLK_DEV), 0, Q)
        owners.append(block_owner.reshape(-1).astype(jnp.int32))
        offsets.append(offset.reshape(-1).astype(jnp.int32))
        levels.append(weight_level.reshape(-1).astype(jnp.int32))
    return (jnp.stack(owners), jnp.stack(offsets), jnp.stack(levels))


def draw_dep_owner(key, part):
    return departures(jax.random.fold_in(key, 11))[0]


def draw_dep_offset(key, part):
    return departures(jax.random.fold_in(key, 11))[1]


def draw_dep_weight(key, part):
    return departures(jax.random.fold_in(key, 11))[2]


def shard_levels(own_key, extent, cuts, smallest, high):
    loudness = 1.0
    for axis_at, shards_of in cuts:
        heights = jax.random.uniform(jax.random.fold_in(jax.random.fold_in(own_key, 6), axis_at), (shards_of,), jnp.float32, smallest / len(cuts), high / len(cuts))
        loudness = loudness * jnp.repeat(jnp.exp(heights), extent[axis_at] // shards_of).reshape((-1,) + (1,) * (len(extent) - 1 - axis_at))
    return loudness


def centred(own_key, extent, spread, reach, cuts=(), kind=jnp.bfloat16):
    drawn = jax.random.normal(own_key, extent, jnp.float32) * spread
    if len(cuts) > 0:
        drawn = shard_levels(own_key, extent, cuts, -0.22, 0.18) * drawn
    return jnp.clip(drawn, min=-reach, max=reach).astype(kind)


def setup_inputs(seed: int = 0, part: int = 0) -> dict:
    arg_keys = jax.random.split(jax.random.key(seed), 7)
    own_keys = jax.random.split(jax.random.fold_in(arg_keys[6], part), 7)
    return {
        "template": draw_template(jax.random.fold_in(jax.random.fold_in(arg_keys[6], part), 71), part),
        "reference_image": draw_reference_image(jax.random.fold_in(jax.random.fold_in(arg_keys[6], part), 71), part),
        "velocity": centred(own_keys[2], (3, NX, NZ, NY), 1.0, 4.0, ((1, 128),), jnp.float32),
        "dep_owner": draw_dep_owner(jax.random.fold_in(jax.random.fold_in(arg_keys[6], part), 71), part),
        "dep_offset": draw_dep_offset(jax.random.fold_in(jax.random.fold_in(arg_keys[6], part), 71), part),
        "dep_weight": draw_dep_weight(jax.random.fold_in(jax.random.fold_in(arg_keys[6], part), 71), part),
    }


h1_weight = 64.0
force_gain = 32.0


def dft_tables(length):
    series = jnp.arange(length, dtype=jnp.int32)
    product = (series[:, None] * series[None, :]) % length
    angles = product.astype(jnp.float32) * (2.0 * math.pi / length)
    return jnp.cos(angles).astype(jnp.bfloat16), jnp.sin(angles).astype(jnp.bfloat16)


def wave_numbers(length):
    series = jnp.arange(length, dtype=jnp.int32)
    signed = jnp.where(series < length // 2, series, series - length)
    signed = jnp.where(series == length // 2, 0, signed)
    return signed.astype(jnp.float32) * (2.0 * math.pi / length)


def cubic_table(levels):
    fraction = (jnp.arange(levels, dtype=jnp.float32) + 0.5) / levels
    node_left = -fraction * (fraction - 1.0) * (fraction - 2.0) / 6.0
    node_zero = (fraction + 1.0) * (fraction - 1.0) * (fraction - 2.0) / 2.0
    node_one = -(fraction + 1.0) * fraction * (fraction - 2.0) / 2.0
    node_two = (fraction + 1.0) * fraction * (fraction - 1.0) / 6.0
    return jnp.stack([node_left, node_zero, node_one, node_two], axis=1)


def transport(grid_field, block_owner, offset, weight_level, weight_table):
    z_groups = NZ // ZB
    y_groups = NY // SEG
    per_row = z_groups * y_groups
    blocks = grid_field.reshape(NX, z_groups, ZB, y_groups, SEG).transpose(0, 1, 3, 2, 4).reshape(NX * per_row, ZB, SEG)
    base_row = block_owner * ROWS + offset // per_row
    remainder = offset % per_row
    tap_rows = (base_row[:, None] + jnp.arange(4, dtype=jnp.int32)[None, :]) % NX
    picked = blocks[tap_rows * per_row + remainder[:, None]].astype(jnp.float32)
    weights = weight_table[weight_level]
    mixed = jnp.sum(weights[:, :, None, None] * picked, axis=1).astype(jnp.bfloat16)
    return mixed.reshape(NX, z_groups, y_groups, ZB, SEG).transpose(0, 1, 3, 2, 4).reshape(NX, NZ, NY)


def reference(template, reference_image, velocity, dep_owner, dep_offset, dep_weight):
    weight_table = cubic_table(Q)
    first_pass = transport(template, dep_owner[0], dep_offset[0], dep_weight[0], weight_table)
    warped = transport(first_pass, dep_owner[1], dep_offset[1], dep_weight[1], weight_table)
    warped_f = warped.astype(jnp.float32)
    residual = reference_image.astype(jnp.float32) - warped_f
    cos_y, sin_y = dft_tables(NY)
    cos_x, sin_x = dft_tables(NX)
    kvec_y = wave_numbers(NY)
    kvec_x = wave_numbers(NX)
    forward_y = jnp.concatenate([cos_y, -sin_y], axis=1)
    inverse_y = jnp.concatenate([cos_y, -sin_y], axis=0)
    forward_x = jnp.concatenate([cos_x, -sin_x], axis=0)
    inverse_x = jnp.concatenate([cos_x, -sin_x], axis=1)
    stack_x = jnp.concatenate([cos_x, sin_x], axis=0)

    spec_y = jnp.dot(warped.reshape(-1, NY), forward_y, preferred_element_type=jnp.float32)
    spec_y = spec_y.astype(jnp.bfloat16).astype(jnp.float32)
    coef_y = jnp.concatenate([-kvec_y * spec_y[:, NY:], kvec_y * spec_y[:, :NY]], axis=1).astype(jnp.bfloat16)
    slope_y = (jnp.dot(coef_y, inverse_y, preferred_element_type=jnp.float32) / NY).reshape(NX, NZ, NY)

    spec_x = jnp.dot(forward_x, warped.reshape(NX, NZ * NY), preferred_element_type=jnp.float32)
    coef_x = jnp.concatenate([-kvec_x[:, None] * spec_x[NX:], kvec_x[:, None] * spec_x[:NX]], axis=0).astype(jnp.bfloat16)
    slope_x = (jnp.dot(inverse_x, coef_x, preferred_element_type=jnp.float32) / NX).astype(jnp.bfloat16).reshape(NX, NZ, NY)

    slope_z = (jnp.roll(warped_f, -1, axis=1) - jnp.roll(warped_f, 1, axis=1)) * 0.5
    force = (jnp.stack([slope_x.astype(jnp.float32), slope_y, slope_z]) * residual[None]).astype(jnp.bfloat16)
    spec_f = jnp.dot(force.reshape(-1, NY), forward_y, preferred_element_type=jnp.float32)
    spec_f = spec_f.astype(jnp.bfloat16).reshape(3, NX, NZ, 2, NY)
    spectral_gain = force_gain / (NX * NY * (1.0 + h1_weight * (kvec_x[:, None] * kvec_x[:, None] + kvec_y[None, :] * kvec_y[None, :])))

    def smooth_component(component):
        halves = jnp.dot(stack_x, component.reshape(NX, -1), preferred_element_type=jnp.float32).reshape(2, NX, NZ, 2, NY)
        real_f = halves[0, :, :, 0] + halves[1, :, :, 1]
        imag_f = halves[0, :, :, 1] - halves[1, :, :, 0]
        scaled = jnp.stack([real_f * spectral_gain[:, None, :], imag_f * spectral_gain[:, None, :]], axis=2).astype(jnp.bfloat16)
        inverse_halves = jnp.dot(stack_x, scaled.reshape(NX, -1), preferred_element_type=jnp.float32).reshape(2, NX, NZ, 2, NY)
        real_b = inverse_halves[0, :, :, 0] - inverse_halves[1, :, :, 1]
        imag_b = inverse_halves[0, :, :, 1] + inverse_halves[1, :, :, 0]
        mixed = jnp.stack([real_b, imag_b], axis=2).astype(jnp.bfloat16)
        return jnp.dot(mixed.reshape(-1, 2 * NY), inverse_y, preferred_element_type=jnp.float32).reshape(NX, NZ, NY)

    smoothed = lax.map(smooth_component, spec_f)
    gradient = velocity + smoothed
    return warped, gradient
```

```python
import math

import jax
import jax.numpy as jnp
import numpy as np
from jax import lax
from jax.sharding import PartitionSpec as P

Q = 16
N = 512
H1_WEIGHT = 64.0
FORCE_GAIN = 32.0


def wave_numbers():
    k = np.arange(N)
    signed = np.where(k < N // 2, k, k - N)
    signed = np.where(k == N // 2, 0, signed)
    return signed * (2.0 * math.pi / N)


def derivative_matrix():
    k = np.arange(N)
    lag = np.arange(N)
    row = (np.sin(2.0 * math.pi * ((k[:, None] * lag[None, :]) % N) / N) * wave_numbers()[:, None]).sum(0) / N
    return row[(lag[None, :] - lag[:, None]) % N]


def basis(points):
    k = np.concatenate([np.arange(N // 2 + 1), np.arange(1, N // 2)])
    angle = 2.0 * math.pi * ((k[:, None] * points[None, :]) % N) / N
    is_cos = (np.arange(N) <= N // 2)[:, None]
    return np.where(is_cos, np.cos(angle), np.sin(angle))


def basis_waves():
    k = np.concatenate([np.arange(N // 2 + 1), np.arange(1, N // 2)])
    weight = np.where((k == 0) | (k == N // 2), 1.0, 2.0)
    return wave_numbers()[k], weight


def bf(x):
    return jnp.asarray(np.asarray(x, np.float32), jnp.bfloat16)


def cubic(level):
    t = (level.astype(jnp.float32) + 0.5) / Q
    return [
        -t * (t - 1.0) * (t - 2.0) / 6.0,
        (t + 1.0) * (t - 1.0) * (t - 2.0) / 2.0,
        -(t + 1.0) * t * (t - 2.0) / 2.0,
        (t + 1.0) * t * (t - 1.0) / 6.0,
    ]


def dot(a, b, dims=((1,), (0,))):
    return lax.dot_general(a, b, (dims, ((), ())), preferred_element_type=jnp.float32)


def transport_matrix(rel, weights):
    row = lax.broadcasted_iota(jnp.int32, (N, N), 0)
    col = lax.broadcasted_iota(jnp.int32, (N, N), 1)
    lag = (col - (row // 4) * 4 - rel.astype(jnp.int32)) & (N - 1)
    out = jnp.zeros((N, N), jnp.bfloat16)
    for tap in range(4):
        out = jnp.where(lag == tap, weights[tap], out)
    return out


def local(template, reference_image, velocity, dep_owner, dep_offset, dep_weight):
    me = lax.axis_index("pencil")
    quarter = me % 4
    plane_even = (me // 4) % 2 == 0
    bf16 = jnp.bfloat16

    move = (dep_owner - me + 130) % 128 - 2
    rel = move * 4 + dep_offset // 64
    codes = []
    for section in range(2):
        codes.append(rel[section].astype(bf16))
        taps = cubic(dep_weight[section])
        high = [w.astype(bf16) for w in taps]
        low = [(w - h.astype(jnp.float32)).astype(bf16) for w, h in zip(taps, high)]
        codes += high + low
    codes = jnp.stack(codes, axis=0).reshape(18, 4, 16, 4).transpose(2, 3, 1, 0)
    codes = jnp.repeat(codes, 2, axis=0)

    def partner(a):
        return a.reshape((16, 2) + a.shape[1:])[:, ::-1].reshape(a.shape)

    def other(a):
        return jnp.roll(partner(jnp.roll(a, 1, axis=0)), -1, axis=0)

    pad = jnp.zeros((32, 4, 4, 46), bf16)
    codes = jnp.concatenate([codes, pad, other(codes), pad], axis=3)
    planes = template.reshape(4, 32, 4, 128).transpose(1, 2, 0, 3)
    image = reference_image.reshape(4, 32, 4, 128).transpose(1, 2, 0, 3)
    pack = jnp.stack(
        [planes, partner(planes), other(planes)]
        + [jnp.roll(image, -s, axis=1) for s in range(4)]
        + [codes],
        axis=2,
    ).reshape(1024, 4, 128)
    got = lax.all_to_all(pack, "pencil", 0, 0, tiled=True).reshape(128, 8, 4, 128)
    unit = [got[:, u].reshape(N, 128) for u in range(8)]

    own = jnp.concatenate([unit[0], unit[1]], axis=1)
    far = unit[2]
    for section in range(2):
        for is_far in range(2):
            at = 64 * is_far + 9 * section
            rel_x = unit[7][:, at : at + 1]
            high = transport_matrix(rel_x, [unit[7][:, at + 1 + k : at + 2 + k] for k in range(4)])
            low = transport_matrix(rel_x, [unit[7][:, at + 5 + k : at + 6 + k] for k in range(4)])
            f = far if is_far else own
            f = (dot(high, f) + dot(low, f)).astype(bf16)
            if is_far:
                far = f
            else:
                own = f
    warped = own[:, :128]
    up = own[:, 128:].astype(jnp.float32) - far.astype(jnp.float32)
    slope_z = up * jnp.where(plane_even, 0.5, -0.5)
    force_z = ((unit[3].astype(jnp.float32) - warped.astype(jnp.float32)) * slope_z).astype(bf16)

    payload = jnp.stack([warped, force_z])
    parts = [payload]
    for s in (1, 2, 3):
        parts.append(
            lax.ppermute(payload, "pencil", [((i // 4) * 4 + (i + s) % 4, i) for i in range(128)])
        )
    whole = jnp.concatenate([p[0] for p in parts], axis=1)
    force_z = jnp.concatenate([p[1] for p in parts], axis=1)
    image = jnp.concatenate([unit[3 + s] for s in range(4)], axis=1)

    deriv = bf(derivative_matrix())
    residual = image.astype(jnp.float32) - whole.astype(jnp.float32)
    force_x = (residual * dot(deriv, whole)).astype(bf16)
    force_y = (residual * dot(whole, deriv, ((1,), (1,)))).astype(bf16)

    table = bf(basis(np.arange(N)))
    mine = lax.dynamic_slice(table, (quarter * 128, 0), (128, N))
    spec = jnp.concatenate(
        [dot(f, mine, ((1,), (1,))).astype(bf16) for f in (force_x, force_y, force_z)], axis=1
    )
    waves, weight = basis_waves()
    wave_x = jnp.asarray(waves, jnp.float32)[:, None]
    wave_y = lax.dynamic_slice(jnp.asarray(waves, jnp.float32), (quarter * 128,), (128,))[None, :]
    scale_x = jnp.asarray(weight * FORCE_GAIN / (N * N), jnp.float32)[:, None]
    scale_y = lax.dynamic_slice(jnp.asarray(weight, jnp.float32), (quarter * 128,), (128,))[None, :]
    gain = scale_x * scale_y / (1.0 + H1_WEIGHT * (wave_x * wave_x + wave_y * wave_y))
    bent = (dot(table, spec) * jnp.concatenate([gain] * 3, axis=1)).astype(bf16)
    back = dot(table, bent, ((0,), (0,))).astype(bf16)

    send = jnp.stack(
        [back[:, 128 * c : 128 * c + 128].reshape(128, 4, 128) for c in range(3)]
        + [warped.reshape(128, 4, 128)],
        axis=1,
    ).reshape(N, 4, 128)
    home = lax.all_to_all(send, "pencil", 0, 0, tiled=True).reshape(32, 4, 4, 4, 128)
    out_warped = home[:, :, 3].transpose(2, 0, 1, 3).reshape(4, 32, N)
    coef = home[:, :, :3].transpose(2, 3, 0, 1, 4).reshape(384, N)
    inverse = np.concatenate([basis((np.arange(N) - 128 * q) % N)[128 * q : 128 * q + 128] for q in range(4)])
    spatial = dot(coef, bf(inverse))
    gradient = velocity + spatial.reshape(3, 4, 32, N)
    return out_warped, gradient


def solution(mesh):
    in_specs = (
        P("pencil", "start", None),
        P("pencil", "start", None),
        P("start", "pencil", None, None),
        P("start", "pencil"),
        P("start", "pencil"),
        P("start", "pencil"),
    )
    out_specs = (P("pencil", "start", None), P("start", "pencil", None, None))
    return jax.shard_map(local, mesh=mesh, in_specs=in_specs, out_specs=out_specs, check_vma=False)
```

```python
import math

import jax
import jax.numpy as jnp
import numpy as np
from jax import lax
from jax.experimental import pallas as pl
from jax.experimental.pallas import tpu as pltpu
from jax.sharding import PartitionSpec as P

Q = 16
N = 512
H1_WEIGHT = 64.0
FORCE_GAIN = 32.0
ROWS = 24
BF = jnp.bfloat16
F32 = jnp.float32
NN = ((1,), (0,))
NT = ((1,), (1,))


def wave_numbers():
    k = np.arange(N)
    signed = np.where(k < N // 2, k, k - N)
    signed = np.where(k == N // 2, 0, signed)
    return signed * (2.0 * math.pi / N)


def derivative_matrix():
    k = np.arange(N)
    lag = np.arange(N)
    row = (np.sin(2.0 * math.pi * ((k[:, None] * lag[None, :]) % N) / N) * wave_numbers()[:, None]).sum(0) / N
    return row[(lag[None, :] - lag[:, None]) % N]


def modes():
    return np.concatenate([np.arange(N // 2 + 1), np.arange(1, N // 2)])


def basis(points):
    angle = 2.0 * math.pi * ((modes()[:, None] * points[None, :]) % N) / N
    is_cos = (np.arange(N) <= N // 2)[:, None]
    return np.where(is_cos, np.cos(angle), np.sin(angle))


def pack_rows():
    pick = np.zeros((32, ROWS // 4, 4, 384), np.float32)
    for z in range(32):
        other = (z + (1 if z % 2 else -1)) % 32
        for x in range(4):
            pick[z, 0, x, x * 32 + z] = 1
            pick[z, 1, x, x * 32 + (z ^ 1)] = 1
            pick[z, 2, x, x * 32 + other] = 1
            pick[z, 3, x, 128 + x * 32 + z] = 1
            pick[z, 4, x, 256 + z * 4 + x] = 1
    return pick.reshape(32 * ROWS, 384)


def bf(x):
    return jnp.asarray(np.asarray(x, np.float32), BF)


def dot(a, b, dims=NN):
    return lax.dot_general(a, b, (dims, ((), ())), preferred_element_type=F32)


def iota(shape, axis):
    return lax.broadcasted_iota(jnp.int32, shape, axis)


def cubic(level):
    t = (level + 0.5) / Q
    return [
        -t * (t - 1.0) * (t - 2.0) / 6.0,
        (t + 1.0) * (t - 1.0) * (t - 2.0) / 2.0,
        -(t + 1.0) * t * (t - 2.0) / 2.0,
        (t + 1.0) * t * (t - 1.0) / 6.0,
    ]


def pack_kernel(me_ref, template_ref, image_ref, owner_ref, offset_ref, weight_ref, pick_ref, out_ref):
    me = me_ref[0]
    move = ((owner_ref[...] - me + 130) & 127) - 2
    rel = (move * 4 + (offset_ref[...] >> 6)).astype(F32)
    level = weight_ref[...].astype(F32)
    row = iota((128, 256), 0)
    second = ((row >> 4) & 1) == 1
    rel = jnp.where(second, rel[1:2], rel[0:1])
    taps = cubic(jnp.where(second, level[1:2], level[0:1]))
    item = row & 15
    value = jnp.where(item == 0, rel, 0.0)
    for k in range(4):
        high = taps[k].astype(BF).astype(F32)
        value = jnp.where(item == 1 + k, high, value)
        value = jnp.where(item == 5 + k, taps[k] - high, value)
    near = jnp.where(row < 32, value, 0.0).astype(BF)
    far = jnp.where((row >= 32) & (row < 64), value, 0.0).astype(BF)
    col = iota((128, 256), 1)
    z = row >> 2
    other = (z + 2 * (z & 1) - 1) & 31
    at_near = (row & 3) * 64 + (z >> 1) * 4
    at_far = (row & 3) * 64 + (other >> 1) * 4
    template = template_ref[...].reshape(128, N)
    image = image_ref[...].reshape(128, N)
    pick = pick_ref[...]
    for q in range(4):
        lanes = slice(128 * q, 128 * q + 128)
        hot_near = jnp.where(col == at_near + q, 1.0, 0.0).astype(BF)
        hot_far = jnp.where(col == at_far + q, 1.0, 0.0).astype(BF)
        codes = (dot(hot_near, near, NT) + dot(hot_far, far, NT)).astype(BF)
        stack = jnp.concatenate([template[:, lanes], image[:, lanes], codes], axis=0)
        out_ref[:, q] = dot(pick, stack).reshape(32, ROWS, 128).astype(BF)


def split(v):
    v = v.reshape(64, 2, 8, 128)
    a, b = v[:, 0], v[:, 1]
    low = iota((64, 8, 128), 1) < 4
    first = jnp.where(low, a, pltpu.roll(b, 4, 1))
    last = jnp.where(low, pltpu.roll(a, 4, 1), b)
    return first.reshape(N, 128), last.reshape(N, 128)


def fill(high_ref, low_ref, codes, at):
    for i in range(4):
        part = codes[128 * i : 128 * i + 128]
        rel = part[:, at : at + 1]
        high = [part[:, at + 1 + k : at + 2 + k] for k in range(4)]
        low = [part[:, at + 5 + k : at + 6 + k] for k in range(4)]
        for tile, first, count in ((0, 0, 128), (-1, 0, 16), (1, 112, 16)):
            rows = slice(first, first + count)
            row = iota((count, 128), 0) + first
            lag = (iota((count, 128), 1) + 128 * tile - (row & -4)).astype(F32) - rel[rows]
            h = jnp.zeros((count, 128), F32)
            l = h
            for k in range(4):
                h = jnp.where(lag == k, high[k][rows], h)
                l = jnp.where(lag == k, low[k][rows], l)
            j = (i + tile) % 4
            where = (slice(128 * i + first, 128 * i + first + count), slice(128 * j, 128 * j + 128))
            high_ref[where] = h.astype(BF)
            low_ref[where] = l.astype(BF)


def transport_kernel(sign_ref, got_ref, out_ref, high_a, low_a, high_b, low_b):
    for ref in (high_a, low_a, high_b, low_b):
        ref[...] = jnp.zeros((N, N), BF)
    own, partner = split(got_ref[:, 0:8, :].astype(F32))
    other, image = split(got_ref[:, 8:16, :].astype(F32))
    codes, _ = split(got_ref[:, 16:24, :].astype(F32))
    near = jnp.concatenate([own, partner], axis=1).astype(BF)
    other = other.astype(BF)
    for section in range(2):
        fill(high_a, low_a, codes, 16 * section)
        fill(high_b, low_b, codes, 32 + 16 * section)
        near = (dot(high_a[...], near) + dot(low_a[...], near)).astype(BF)
        other = (dot(high_b[...], other) + dot(low_b[...], other)).astype(BF)
    warped = near[:, :128]
    slope = (near[:, 128:].astype(F32) - other.astype(F32)) * sign_ref[0]
    out_ref[0] = warped
    out_ref[1] = image.astype(BF)
    out_ref[2] = ((image - warped.astype(F32)) * slope).astype(BF)


def smooth_kernel(quarter_ref, p0_ref, p1_ref, p2_ref, p3_ref, deriv_ref, table_ref, flip_ref, wave_ref, wy_ref, out_ref):
    parts = (p0_ref, p1_ref, p2_ref, p3_ref)
    warped = jnp.concatenate([p[0] for p in parts], axis=1)
    deriv = deriv_ref[...]
    mine = flip_ref[:, pl.ds(pl.multiple_of(quarter_ref[0] * 128, 128), 128)]
    slope_x = dot(deriv, warped)
    slope_y = dot(warped, deriv)
    image = jnp.concatenate([p[1] for p in parts], axis=1).astype(F32)
    residual = image - warped.astype(F32)
    force_x = (residual * slope_x).astype(BF)
    force_y = (residual * (-slope_y)).astype(BF)
    force_z = jnp.concatenate([p[2] for p in parts], axis=1)
    spec = jnp.concatenate([dot(f, mine).astype(BF) for f in (force_x, force_y, force_z)], axis=1)
    wave_x = wave_ref[:, 0:1]
    scale_x = wave_ref[:, 1:2]
    gain = (scale_x * wy_ref[1:2]) / (1.0 + H1_WEIGHT * (wave_x * wave_x + wy_ref[0:1] * wy_ref[0:1]))
    bent = dot(table_ref[...], spec)
    bent = jnp.concatenate([bent[:, 128 * c : 128 * c + 128] * gain for c in range(3)], axis=1).astype(BF)
    back = dot(flip_ref[...], bent)
    a = [back[:, 128 * c : 128 * c + 128].reshape(64, 8, 128) for c in range(3)]
    a.append(warped[:, :128].astype(F32).reshape(64, 8, 128))
    low = iota((64, 8, 128), 1) < 4
    turned = [pltpu.roll(v, 4, 1) for v in a]
    even = [jnp.where(low, a[j], turned[j + 1]) for j in (0, 2)]
    odd = [jnp.where(low, turned[j], a[j + 1]) for j in (0, 2)]
    out_ref[:, 0] = jnp.concatenate(even, axis=1).astype(BF)
    out_ref[:, 1] = jnp.concatenate(odd, axis=1).astype(BF)


def call(kernel, out, scratch=(), scalars=1, inputs=1):
    return pl.pallas_call(
        kernel,
        out_shape=jax.ShapeDtypeStruct(out, BF),
        in_specs=[pl.BlockSpec(memory_space=pltpu.SMEM)] * scalars
        + [pl.BlockSpec(memory_space=pltpu.VMEM)] * inputs,
        out_specs=pl.BlockSpec(memory_space=pltpu.VMEM),
        scratch_shapes=list(scratch),
        compiler_params=pltpu.CompilerParams(vmem_limit_bytes=48 << 20),
    )


def local(template, reference_image, velocity, dep_owner, dep_offset, dep_weight):
    me = lax.axis_index("pencil")
    quarter = me % 4
    sign = jnp.where((me // 4) % 2 == 0, 0.5, -0.5).astype(F32)

    pack = call(pack_kernel, (32, 4, ROWS, 128), inputs=6)(
        me.reshape(1), template, reference_image, dep_owner, dep_offset, dep_weight, bf(pack_rows())
    )
    got = lax.all_to_all(pack.reshape(128, ROWS, 128), "pencil", 0, 0, tiled=True)

    payload = call(transport_kernel, (3, N, 128), scratch=[pltpu.VMEM((N, N), BF)] * 4)(
        sign.reshape(1), got
    )
    parts = [payload]
    for s in (1, 2, 3):
        parts.append(
            lax.ppermute(payload, "pencil", [((i // 4) * 4 + (i + s) % 4, i) for i in range(128)])
        )

    table = basis(np.arange(N))
    k = modes()
    wave = wave_numbers()[k]
    weight = np.where((k == 0) | (k == N // 2), 1.0, 2.0)
    wave_x = np.zeros((N, 128), np.float32)
    wave_x[:, 0] = wave
    wave_x[:, 1] = weight * FORCE_GAIN / (N * N)
    wave_y = np.zeros((4, 8, 128), np.float32)
    wave_y[:, 0] = wave.reshape(4, 128)
    wave_y[:, 1] = weight.reshape(4, 128)
    wave_y = lax.dynamic_index_in_dim(jnp.asarray(wave_y), quarter, keepdims=False)
    send = call(smooth_kernel, (64, 2, 16, 128), inputs=9)(
        quarter.reshape(1), *parts, bf(derivative_matrix()), bf(table), bf(table.T), jnp.asarray(wave_x), wave_y
    )
    home = lax.all_to_all(send.reshape(128, 16, 128), "pencil", 0, 0, tiled=True)

    rows = home.reshape(32, 4, 16, 128).transpose(0, 2, 1, 3).reshape(N, N)
    target = np.zeros((N, N), np.float32)
    r = np.arange(N)
    target[r, (r % 32) * 16 + r // 32] = 1
    rows = dot(bf(target), rows).astype(BF)
    inverse = np.concatenate([basis((np.arange(N) - 128 * q) % N)[128 * q : 128 * q + 128] for q in range(4)])
    spatial = dot(rows[:384], bf(inverse))
    return rows[384:].reshape(4, 32, N), velocity + spatial.reshape(3, 4, 32, N)


def solution(mesh):
    in_specs = (
        P("pencil", "start", None),
        P("pencil", "start", None),
        P("start", "pencil", None, None),
        P("start", "pencil"),
        P("start", "pencil"),
        P("start", "pencil"),
    )
    out_specs = (P("pencil", "start", None), P("start", "pencil", None, None))
    return jax.shard_map(local, mesh=mesh, in_specs=in_specs, out_specs=out_specs, check_vma=False)
```

```python
import math

import jax
import jax.numpy as jnp
import numpy as np
from jax import lax
from jax.experimental import pallas as pl
from jax.experimental.pallas import tpu as pltpu
from jax.sharding import PartitionSpec as P

Q = 16
N = 512
H1_WEIGHT = 64.0
FORCE_GAIN = 32.0
BF = jnp.bfloat16
F32 = jnp.float32
NN = ((1,), (0,))
NT = ((1,), (1,))


def wave_numbers():
    k = np.arange(N)
    signed = np.where(k < N // 2, k, k - N)
    signed = np.where(k == N // 2, 0, signed)
    return signed * (2.0 * math.pi / N)


def derivative_matrix():
    k = np.arange(N)
    lag = np.arange(N)
    row = (np.sin(2.0 * math.pi * ((k[:, None] * lag[None, :]) % N) / N) * wave_numbers()[:, None]).sum(0) / N
    return row[(lag[None, :] - lag[:, None]) % N]


def modes():
    return np.concatenate([np.arange(N // 2 + 1), np.arange(1, N // 2)])


def basis(points):
    angle = 2.0 * math.pi * ((modes()[:, None] * points[None, :]) % N) / N
    is_cos = (np.arange(N) <= N // 2)[:, None]
    return np.where(is_cos, np.cos(angle), np.sin(angle))


def pack_rows():
    pick = np.zeros((32, 6, 4, 384), np.float32)
    for z in range(32):
        other = (z + (1 if z % 2 else -1)) % 32
        for x in range(4):
            pick[z, 0, x, x * 32 + z] = 1
            pick[z, 1, x, x * 32 + (z ^ 1)] = 1
            pick[z, 2, x, x * 32 + other] = 1
            pick[z, 3, x, 128 + x * 32 + z] = 1
            pick[z, 4, x, 256 + z * 4 + x] = 1
            pick[z, 5, x, 256 + z * 4 + x] = 1
    return pick.reshape(768, 384)


def unpack_rows():
    r = np.arange(N)
    pick = np.zeros((N, N), np.float32)
    pick[r, (r % 32) * 16 + (r // 128) * 4 + (r // 32) % 4] = 1
    return pick


def bf(x):
    return jnp.asarray(np.asarray(x, np.float32), BF)


def dot(a, b, dims=NN):
    return lax.dot_general(a, b, (dims, ((), ())), preferred_element_type=F32)


def iota(shape, axis):
    return lax.broadcasted_iota(jnp.int32, shape, axis)


def cubic(level):
    t = (level + 0.5) / Q
    return [
        -t * (t - 1.0) * (t - 2.0) / 6.0,
        (t + 1.0) * (t - 1.0) * (t - 2.0) / 2.0,
        -(t + 1.0) * t * (t - 2.0) / 2.0,
        (t + 1.0) * t * (t - 1.0) / 6.0,
    ]


def mode_waves(shape, axis):
    i = iota(shape, axis)
    k = jnp.where(i < N // 2, i, i - N // 2)
    wave = k.astype(F32) * (2.0 * math.pi / N)
    return wave, jnp.where(k == 0, 1.0, 2.0)


def fetch(refs, scratch, sem):
    copies = [pltpu.make_async_copy(r, v, sem.at[i]) for i, (r, v) in enumerate(zip(refs, scratch))]
    for copy in copies:
        copy.start()
    return copies


def pack_kernel(owner_ref, offset_ref, weight_ref, template_ref, image_ref, pick_ref, out_ref, owner, offset, weight, template, image, pick, sem):
    copies = fetch(
        (owner_ref, offset_ref, weight_ref, template_ref, image_ref, pick_ref),
        (owner, offset, weight, template, image, pick),
        sem,
    )
    me = lax.axis_index("pencil")
    for copy in copies[:3]:
        copy.wait()
    move = ((owner[...] - me + 130) & 127) - 2
    rel = (move * 4 + (offset[...] >> 6)).astype(F32)
    level = weight[...].astype(F32)
    row = iota((128, 256), 0)
    second = ((row >> 4) & 1) == 1
    rel = jnp.where(second, rel[1:2], rel[0:1])
    taps = cubic(jnp.where(second, level[1:2], level[0:1]))
    item = row & 15
    value = jnp.where(item == 0, rel, 0.0)
    for k in range(4):
        high = taps[k].astype(BF).astype(F32)
        value = jnp.where(item == 1 + k, high, value)
        value = jnp.where(item == 5 + k, taps[k] - high, value)
    near = jnp.where(row < 32, value, 0.0).astype(BF)
    far = jnp.where((row >= 32) & (row < 64), value, 0.0).astype(BF)
    col = iota((128, 256), 1)
    z = row >> 2
    other = (z + 2 * (z & 1) - 1) & 31
    at_near = (row & 3) * 64 + (z >> 1) * 4
    at_far = (row & 3) * 64 + (other >> 1) * 4
    for copy in copies[3:]:
        copy.wait()
    template = template[...].reshape(128, N)
    image = image[...].reshape(128, N)
    pick = pick[...]
    low = iota((32, 8, 128), 1) < 4
    for pair in range(2):
        units = []
        for q in (2 * pair, 2 * pair + 1):
            lanes = slice(128 * q, 128 * q + 128)
            hot_near = jnp.where(col == at_near + q, 1.0, 0.0).astype(BF)
            hot_far = jnp.where(col == at_far + q, 1.0, 0.0).astype(BF)
            codes = (dot(hot_near, near, NT) + dot(hot_far, far, NT)).astype(BF)
            stack = jnp.concatenate([template[:, lanes], image[:, lanes], codes], axis=0)
            rows = dot(pick, stack).reshape(32, 3, 8, 128)
            units += [rows[:, 0], rows[:, 1], rows[:, 2]]
        a, b, c, d, e, f = units
        d, e = pltpu.roll(d, 4, 1), pltpu.roll(e, 4, 1)
        tiles = [a, b, jnp.where(low, c, d), jnp.where(low, d, e), jnp.where(low, e, f)]
        out_ref[:, pair] = jnp.concatenate(tiles, axis=1).astype(BF)


def units_of(ref):
    t = [ref[:, 8 * i : 8 * i + 8, :].astype(F32) for i in range(5)]
    low = iota((64, 8, 128), 1) < 4
    units = [
        jnp.where(low, t[0], t[2]),
        pltpu.roll(jnp.where(low, t[3], t[0]), 4, 1),
        jnp.where(low, t[1], t[3]),
        pltpu.roll(jnp.where(low, t[4], t[1]), 4, 1),
        jnp.where(low, t[2], t[4]),
    ]
    return [u.reshape(N, 128) for u in units]


def units_to(ref, units):
    a, b, c, d, e = [u.reshape(64, 8, 128) for u in units]
    low = iota((64, 8, 128), 1) < 4
    turned_b, turned_d = pltpu.roll(b, 4, 1), pltpu.roll(d, 4, 1)
    tiles = [
        jnp.where(low, a, turned_b),
        jnp.where(low, c, turned_d),
        jnp.where(low, e, a),
        jnp.where(low, turned_b, c),
        jnp.where(low, turned_d, e),
    ]
    ref[...] = jnp.concatenate(tiles, axis=1).astype(BF)


def fill(high_ref, low_ref, codes, at):
    for i in range(4):
        part = codes[128 * i : 128 * i + 128]
        rel = part[:, at : at + 1]
        high = [part[:, at + 1 + k : at + 2 + k] for k in range(4)]
        low = [part[:, at + 5 + k : at + 6 + k] for k in range(4)]
        for tile, first, count in ((0, 0, 128), (-1, 0, 16), (1, 112, 16)):
            rows = slice(first, first + count)
            row = iota((count, 128), 0) + first
            lag = (iota((count, 128), 1) + 128 * tile - (row & -4)).astype(F32) - rel[rows]
            h = jnp.zeros((count, 128), F32)
            l = h
            for k in range(4):
                h = jnp.where(lag == k, high[k][rows], h)
                l = jnp.where(lag == k, low[k][rows], l)
            j = (i + tile) % 4
            where = (slice(128 * i + first, 128 * i + first + count), slice(128 * j, 128 * j + 128))
            high_ref[where] = h.astype(BF)
            low_ref[where] = l.astype(BF)


def transport_kernel(got_ref, deriv_ref, out0_ref, out1_ref, out2_ref, out3_ref, warped_ref, high_a, low_a, high_b, low_b, pieces):
    me = lax.axis_index("pencil")
    for ref in (high_a, low_a, high_b, low_b):
        ref[...] = jnp.zeros((N, N), BF)
    own, partner, other, image, codes = units_of(got_ref)
    near = jnp.concatenate([own, partner], axis=1).astype(BF)
    other = other.astype(BF)
    for section in range(2):
        fill(high_a, low_a, codes, 16 * section)
        fill(high_b, low_b, codes, 32 + 16 * section)
        near = (dot(high_a[...], near) + dot(low_a[...], near)).astype(BF)
        other = (dot(high_b[...], other) + dot(low_b[...], other)).astype(BF)
    warped = near[:, :128]
    residual = image - warped.astype(F32)
    image = image.astype(BF)
    sign = jnp.where((me & 4) == 0, 0.5, -0.5).astype(F32)
    slope_z = (near[:, 128:].astype(F32) - other.astype(F32)) * sign
    warped_ref[...] = warped
    pieces[0] = (residual * dot(deriv_ref[...], warped)).astype(BF)
    pieces[1, 0:256] = warped[0:256]
    pieces[1, 256:512] = image[0:256]
    pieces[2] = (residual * slope_z).astype(BF)
    pieces[3, 0:256] = warped[256:512]
    pieces[3, 256:512] = image[256:512]
    for s, ref in enumerate((out0_ref, out1_ref, out2_ref, out3_ref)):
        ref[...] = pieces[(me - s) & 3]


def smooth_kernel(p0_ref, p1_ref, p2_ref, p3_ref, warped_ref, deriv_ref, table_ref, flip_ref, out_ref, plane, tiles):
    role = lax.axis_index("pencil") & 3
    parts = jnp.concatenate([p[...] for p in (p0_ref, p1_ref, p2_ref, p3_ref)], axis=1)

    @pl.when((role & 1) == 0)
    def _():
        plane[...] = parts

    @pl.when((role & 1) == 1)
    def _():
        half = parts[0:256]
        slope_y = -dot(half, deriv_ref[...])
        force = ((parts[256:512].astype(F32) - half.astype(F32)) * slope_y).astype(BF)
        at = (role >> 1) * 256
        plane[pl.ds(pl.multiple_of(at, 256), 256)] = force
        plane[pl.ds(pl.multiple_of(256 - at, 256), 256)] = jnp.zeros((256, N), BF)

    spec = dot(plane[...], flip_ref[...]).astype(BF)
    wave_x, scale_x = mode_waves((N, 1), 0)
    wave_y, scale_y = mode_waves((1, N), 1)
    gain = (scale_x * scale_y * (FORCE_GAIN / (N * N))) / (1.0 + H1_WEIGHT * (wave_x * wave_x + wave_y * wave_y))
    bent = (dot(table_ref[...], spec) * gain).astype(BF)
    back = dot(flip_ref[...], bent).astype(BF)
    smooth = dot(back, table_ref[...])
    for s in range(4):
        tiles[(role + s) & 3] = smooth[:, 128 * s : 128 * s + 128]
    units_to(out_ref, [tiles[0], tiles[1], tiles[2], tiles[3], warped_ref[...].astype(F32)])


def finish_kernel(home_ref, pick_ref, velocity_ref, out_warped_ref, out_ref, velocity, result, warped, sem):
    loads = fetch([velocity_ref.at[c] for c in range(3)], [velocity.at[c] for c in range(3)], sem)
    pick = pick_ref[...]
    units = units_of(home_ref)
    rows = jnp.concatenate(units[:4], axis=1).astype(BF)
    turned = dot(pick, units[4].astype(BF))
    for r in range(4):
        warped[:, :, 128 * r : 128 * r + 128] = turned[128 * r : 128 * r + 128].reshape(4, 32, 128).astype(BF)
    stores = [pltpu.make_async_copy(warped, out_warped_ref, sem.at[3])]
    stores[0].start()
    for c in range(3):
        which = pick[128 * c : 128 * c + 128]
        if c == 1:
            which = which + pick[384:512]
        part = dot(which, rows).reshape(4, 32, N)
        loads[c].wait()
        result[c] = velocity[c] + part
        store = pltpu.make_async_copy(result.at[c], out_ref.at[c], sem.at[4 + c])
        store.start()
        stores.append(store)
    for store in stores:
        store.wait()


ANY = pl.BlockSpec(memory_space=pl.ANY)
VMEM = pl.BlockSpec(memory_space=pltpu.VMEM)


def call(kernel, outs, in_specs, out_specs, scratch):
    return pl.pallas_call(
        kernel,
        out_shape=outs,
        in_specs=in_specs,
        out_specs=out_specs,
        scratch_shapes=scratch,
        compiler_params=pltpu.CompilerParams(vmem_limit_bytes=48 << 20),
    )


def local(template, reference_image, velocity, dep_owner, dep_offset, dep_weight):
    shape = jax.ShapeDtypeStruct
    piece = shape((N, 128), BF)
    vm = pltpu.VMEM

    pick = bf(pack_rows())
    inputs = (dep_owner, dep_offset, dep_weight, template, reference_image, pick)
    pack = call(
        pack_kernel,
        shape((32, 2, 40, 128), BF),
        [ANY] * 6,
        VMEM,
        [vm(a.shape, a.dtype) for a in inputs] + [pltpu.SemaphoreType.DMA((6,))],
    )(*inputs)
    got = lax.all_to_all(pack.reshape(640, 4, 128), "pencil", 0, 0, tiled=True)

    deriv = bf(derivative_matrix())
    *parts, warped = call(
        transport_kernel,
        [piece] * 5,
        [VMEM] * 2,
        [VMEM] * 5,
        [vm((N, N), BF)] * 4 + [vm((4, N, 128), BF)],
    )(got.reshape(64, 40, 128), deriv)
    for s in (1, 2, 3):
        parts[s] = lax.ppermute(parts[s], "pencil", [((i // 4) * 4 + (i + s) % 4, i) for i in range(128)])

    table = basis(np.arange(N))
    send = call(
        smooth_kernel,
        shape((64, 40, 128), BF),
        [VMEM] * 8,
        VMEM,
        [vm((N, N), BF), vm((4, N, 128), F32)],
    )(*parts, warped, deriv, bf(table), bf(table.T))
    home = lax.all_to_all(send.reshape(640, 4, 128), "pencil", 0, 0, tiled=True)

    return call(
        finish_kernel,
        [shape((4, 32, N), BF), shape((3, 4, 32, N), F32)],
        [VMEM, VMEM, ANY],
        [ANY, ANY],
        [vm((3, 4, 32, N), F32), vm((3, 4, 32, N), F32), vm((4, 32, N), BF), pltpu.SemaphoreType.DMA((7,))],
    )(home.reshape(64, 40, 128), bf(unpack_rows()), velocity)


def solution(mesh):
    in_specs = (
        P("pencil", "start", None),
        P("pencil", "start", None),
        P("start", "pencil", None, None),
        P("start", "pencil"),
        P("start", "pencil"),
        P("start", "pencil"),
    )
    out_specs = (P("pencil", "start", None), P("start", "pencil", None, None))
    return jax.shard_map(local, mesh=mesh, in_specs=in_specs, out_specs=out_specs, check_vma=False)
```

```python
import math

import jax
import jax.numpy as jnp
import numpy as np
from jax import lax
from jax.experimental import pallas as pl
from jax.experimental.pallas import tpu as pltpu
from jax.sharding import PartitionSpec as P

Q = 16
N = 512
H1_WEIGHT = 64.0
FORCE_GAIN = 32.0
BF = jnp.bfloat16
F32 = jnp.float32
NN = ((1,), (0,))
NT = ((1,), (1,))


def wave_numbers():
    k = np.arange(N)
    signed = np.where(k < N // 2, k, k - N)
    signed = np.where(k == N // 2, 0, signed)
    return signed * (2.0 * math.pi / N)


def derivative_matrix():
    k = np.arange(N)
    lag = np.arange(N)
    row = (np.sin(2.0 * math.pi * ((k[:, None] * lag[None, :]) % N) / N) * wave_numbers()[:, None]).sum(0) / N
    return row[(lag[None, :] - lag[:, None]) % N]


def modes():
    return np.concatenate([np.arange(N // 2 + 1), np.arange(1, N // 2)])


def basis(points):
    angle = 2.0 * math.pi * ((modes()[:, None] * points[None, :]) % N) / N
    is_cos = (np.arange(N) <= N // 2)[:, None]
    return np.where(is_cos, np.cos(angle), np.sin(angle))


def pack_rows():
    pick = np.zeros((32, 6, 4, 384), np.float32)
    for z in range(32):
        other = (z + (1 if z % 2 else -1)) % 32
        for x in range(4):
            pick[z, 0, x, x * 32 + z] = 1
            pick[z, 1, x, x * 32 + (z ^ 1)] = 1
            pick[z, 2, x, x * 32 + other] = 1
            pick[z, 3, x, 128 + x * 32 + z] = 1
            pick[z, 4, x, 256 + z * 4 + x] = 1
            pick[z, 5, x, 256 + z * 4 + x] = 1
    return pick.reshape(768, 384)


def unpack_rows():
    r = np.arange(N)
    role, x, z = r // 128, (r // 32) % 4, r % 32
    device = (z // 2) * 8 + (role // 2) * 4 + (z % 2) * 2 + role % 2
    pick = np.zeros((N, N), np.float32)
    pick[r, device * 4 + x] = 1
    return pick


PARTNER = (0, 1, 4, 5)


def quarter_of(device):
    return ((device >> 1) & 2) + (device & 1)


def bf(x):
    return jnp.asarray(np.asarray(x, np.float32), BF)


def dot(a, b, dims=NN):
    return lax.dot_general(a, b, (dims, ((), ())), preferred_element_type=F32)


def iota(shape, axis):
    return lax.broadcasted_iota(jnp.int32, shape, axis)


def cubic(level):
    t = (level + 0.5) / Q
    return [
        -t * (t - 1.0) * (t - 2.0) / 6.0,
        (t + 1.0) * (t - 1.0) * (t - 2.0) / 2.0,
        -(t + 1.0) * t * (t - 2.0) / 2.0,
        (t + 1.0) * t * (t - 1.0) / 6.0,
    ]


def mode_waves(shape, axis):
    i = iota(shape, axis)
    k = jnp.where(i < N // 2, i, i - N // 2)
    wave = k.astype(F32) * (2.0 * math.pi / N)
    return wave, jnp.where(k == 0, 1.0, 2.0)


def fetch(refs, scratch, sem):
    copies = [pltpu.make_async_copy(r, v, sem.at[i]) for i, (r, v) in enumerate(zip(refs, scratch))]
    for copy in copies:
        copy.start()
    return copies


def pack_kernel(owner_ref, offset_ref, weight_ref, template_ref, image_ref, pick_ref, out_ref, owner, offset, weight, template, image, pick, sem):
    copies = fetch(
        (owner_ref, offset_ref, weight_ref, template_ref, image_ref, pick_ref),
        (owner, offset, weight, template, image, pick),
        sem,
    )
    me = lax.axis_index("pencil")
    for copy in copies[:3]:
        copy.wait()
    move = ((owner[...] - me + 130) & 127) - 2
    rel = (move * 4 + (offset[...] >> 6)).astype(F32)
    level = weight[...].astype(F32)
    row = iota((128, 256), 0)
    second = ((row >> 4) & 1) == 1
    rel = jnp.where(second, rel[1:2], rel[0:1])
    taps = cubic(jnp.where(second, level[1:2], level[0:1]))
    item = row & 15
    value = jnp.where(item == 0, rel, 0.0)
    for k in range(4):
        high = taps[k].astype(BF).astype(F32)
        value = jnp.where(item == 1 + k, high, value)
        value = jnp.where(item == 5 + k, taps[k] - high, value)
    near = jnp.where(row < 32, value, 0.0).astype(BF)
    far = jnp.where((row >= 32) & (row < 64), value, 0.0).astype(BF)
    col = iota((128, 256), 1)
    z = row >> 2
    other = (z + 2 * (z & 1) - 1) & 31
    at_near = (row & 3) * 64 + (z >> 1) * 4
    at_far = (row & 3) * 64 + (other >> 1) * 4
    for copy in copies[3:]:
        copy.wait()
    template = template[...].reshape(128, N)
    image = image[...].reshape(128, N)
    pick = pick[...]
    low = iota((32, 8, 128), 1) < 4
    for pair in range(2):
        units = []
        for q in (2 * pair, 2 * pair + 1):
            lanes = slice(128 * q, 128 * q + 128)
            hot_near = jnp.where(col == at_near + q, 1.0, 0.0).astype(BF)
            hot_far = jnp.where(col == at_far + q, 1.0, 0.0).astype(BF)
            codes = (dot(hot_near, near, NT) + dot(hot_far, far, NT)).astype(BF)
            stack = jnp.concatenate([template[:, lanes], image[:, lanes], codes], axis=0)
            rows = dot(pick, stack).reshape(32, 3, 8, 128)
            units += [rows[:, 0], rows[:, 1], rows[:, 2]]
        a, b, c, d, e, f = units
        d, e = pltpu.roll(d, 4, 1), pltpu.roll(e, 4, 1)
        tiles = [a, b, jnp.where(low, c, d), jnp.where(low, d, e), jnp.where(low, e, f)]
        out_ref[:, pair] = jnp.concatenate(tiles, axis=1).astype(BF).reshape(16, 2, 40, 128)


def units_of(ref):
    t = [ref[:, 8 * i : 8 * i + 8, :].astype(F32) for i in range(5)]
    low = iota((64, 8, 128), 1) < 4
    units = [
        jnp.where(low, t[0], t[2]),
        pltpu.roll(jnp.where(low, t[3], t[0]), 4, 1),
        jnp.where(low, t[1], t[3]),
        pltpu.roll(jnp.where(low, t[4], t[1]), 4, 1),
        jnp.where(low, t[2], t[4]),
    ]
    return [u.reshape(N, 128) for u in units]


def units_to(ref, units):
    a, b, c, d, e = [u.reshape(64, 8, 128) for u in units]
    low = iota((64, 8, 128), 1) < 4
    turned_b, turned_d = pltpu.roll(b, 4, 1), pltpu.roll(d, 4, 1)
    tiles = [
        jnp.where(low, a, turned_b),
        jnp.where(low, c, turned_d),
        jnp.where(low, e, a),
        jnp.where(low, turned_b, c),
        jnp.where(low, turned_d, e),
    ]
    ref[...] = jnp.concatenate(tiles, axis=1).astype(BF)


def fill(high_ref, low_ref, codes, at):
    for i in range(4):
        part = codes[128 * i : 128 * i + 128]
        rel = part[:, at : at + 1]
        high = [part[:, at + 1 + k : at + 2 + k] for k in range(4)]
        low = [part[:, at + 5 + k : at + 6 + k] for k in range(4)]
        for tile, first, count in ((0, 0, 128), (-1, 0, 16), (1, 112, 16)):
            rows = slice(first, first + count)
            row = iota((count, 128), 0) + first
            lag = (iota((count, 128), 1) + 128 * tile - (row & -4)).astype(F32) - rel[rows]
            h = jnp.zeros((count, 128), F32)
            l = h
            for k in range(4):
                h = jnp.where(lag == k, high[k][rows], h)
                l = jnp.where(lag == k, low[k][rows], l)
            j = (i + tile) % 4
            where = (slice(128 * i + first, 128 * i + first + count), slice(128 * j, 128 * j + 128))
            high_ref[where] = h.astype(BF)
            low_ref[where] = l.astype(BF)


def transport_kernel(got_ref, deriv_ref, out0_ref, out1_ref, out2_ref, out3_ref, warped_ref, high_a, low_a, high_b, low_b, pieces):
    me = lax.axis_index("pencil")
    for ref in (high_a, low_a, high_b, low_b):
        ref[...] = jnp.zeros((N, N), BF)
    own, partner, other, image, codes = units_of(got_ref)
    near = jnp.concatenate([own, partner], axis=1).astype(BF)
    other = other.astype(BF)
    for section in range(2):
        fill(high_a, low_a, codes, 16 * section)
        fill(high_b, low_b, codes, 32 + 16 * section)
        near = (dot(high_a[...], near) + dot(low_a[...], near)).astype(BF)
        other = (dot(high_b[...], other) + dot(low_b[...], other)).astype(BF)
    warped = near[:, :128]
    residual = image - warped.astype(F32)
    image = image.astype(BF)
    sign = jnp.where((me & 2) == 0, 0.5, -0.5).astype(F32)
    slope_z = (near[:, 128:].astype(F32) - other.astype(F32)) * sign
    warped_ref[...] = warped
    pieces[0] = (residual * dot(deriv_ref[...], warped)).astype(BF)
    pieces[1, 0:256] = warped[0:256]
    pieces[1, 256:512] = image[0:256]
    pieces[2] = (residual * slope_z).astype(BF)
    pieces[3, 0:256] = warped[256:512]
    pieces[3, 256:512] = image[256:512]
    for s, ref in enumerate((out0_ref, out1_ref, out2_ref, out3_ref)):
        ref[...] = pieces[quarter_of(me) ^ s]


def smooth_kernel(p0_ref, p1_ref, p2_ref, p3_ref, warped_ref, deriv_ref, table_ref, flip_ref, out_ref, plane):
    role = quarter_of(lax.axis_index("pencil"))
    for s, ref in enumerate((p0_ref, p1_ref, p2_ref, p3_ref)):
        plane[:, pl.ds(pl.multiple_of((role ^ s) * 128, 128), 128)] = ref[...]

    @pl.when((role & 1) == 1)
    def _():
        half = plane[0:256]
        slope_y = -dot(half, deriv_ref[...])
        force = ((plane[256:512].astype(F32) - half.astype(F32)) * slope_y).astype(BF)
        at = (role >> 1) * 256
        plane[pl.ds(pl.multiple_of(at, 256), 256)] = force
        plane[pl.ds(pl.multiple_of(256 - at, 256), 256)] = jnp.zeros((256, N), BF)

    spec = dot(plane[...], flip_ref[...]).astype(BF)
    wave_x, scale_x = mode_waves((N, 1), 0)
    wave_y, scale_y = mode_waves((1, N), 1)
    gain = (scale_x * scale_y * (FORCE_GAIN / (N * N))) / (1.0 + H1_WEIGHT * (wave_x * wave_x + wave_y * wave_y))
    bent = (dot(table_ref[...], spec) * gain).astype(BF)
    back = dot(flip_ref[...], bent).astype(BF)
    smooth = dot(back, table_ref[...])
    units = [smooth[:, 128 * s : 128 * s + 128] for s in range(4)]
    units_to(out_ref, units + [warped_ref[...].astype(F32)])


def finish_kernel(home_ref, pick_ref, velocity_ref, out_warped_ref, out_ref, velocity, result, warped, sem):
    loads = fetch([velocity_ref.at[c] for c in range(3)], [velocity.at[c] for c in range(3)], sem)
    pick = pick_ref[...]
    units = units_of(home_ref)
    rows = jnp.concatenate(units[:4], axis=1).astype(BF)
    turned = dot(pick, units[4].astype(BF))
    for r in range(4):
        warped[:, :, 128 * r : 128 * r + 128] = turned[128 * r : 128 * r + 128].reshape(4, 32, 128).astype(BF)
    stores = [pltpu.make_async_copy(warped, out_warped_ref, sem.at[3])]
    stores[0].start()
    for c in range(3):
        which = pick[128 * c : 128 * c + 128]
        if c == 1:
            which = which + pick[384:512]
        part = dot(which, rows).reshape(4, 32, N)
        loads[c].wait()
        result[c] = velocity[c] + part
        store = pltpu.make_async_copy(result.at[c], out_ref.at[c], sem.at[4 + c])
        store.start()
        stores.append(store)
    for store in stores:
        store.wait()


ANY = pl.BlockSpec(memory_space=pltpu.HBM)
VMEM = pl.BlockSpec(memory_space=pltpu.VMEM)


def call(kernel, outs, in_specs, out_specs, scratch, grant=48 << 20):
    return pl.pallas_call(
        kernel,
        out_shape=outs,
        in_specs=in_specs,
        out_specs=out_specs,
        scratch_shapes=scratch,
        compiler_params=pltpu.CompilerParams(vmem_limit_bytes=grant),
    )


def local(template, reference_image, velocity, dep_owner, dep_offset, dep_weight):
    shape = jax.ShapeDtypeStruct
    piece = shape((N, 128), BF)
    vm = pltpu.VMEM

    pick = bf(pack_rows())
    inputs = (dep_owner, dep_offset, dep_weight, template, reference_image, pick)
    pack = call(
        pack_kernel,
        shape((16, 2, 2, 40, 128), BF),
        [ANY] * 6,
        VMEM,
        [vm(a.shape, a.dtype) for a in inputs] + [pltpu.SemaphoreType.DMA((6,))],
        65000000,
    )(*inputs)
    got = lax.all_to_all(pack.reshape(640, 4, 128), "pencil", 0, 0, tiled=True)

    deriv = bf(derivative_matrix())
    *parts, warped = call(
        transport_kernel,
        [piece] * 5,
        [VMEM] * 2,
        [VMEM] * 5,
        [vm((N, N), BF)] * 4 + [vm((4, N, 128), BF)],
    )(got.reshape(64, 40, 128), deriv)
    for s in (1, 2, 3):
        parts[s] = lax.ppermute(parts[s], "pencil", [(i ^ PARTNER[s], i) for i in range(128)])

    table = basis(np.arange(N))
    send = call(
        smooth_kernel,
        shape((64, 40, 128), BF),
        [VMEM] * 8,
        VMEM,
        [vm((N, N), BF)],
    )(*parts, warped, deriv, bf(table), bf(table.T))
    home = lax.all_to_all(send.reshape(640, 4, 128), "pencil", 0, 0, tiled=True)

    return call(
        finish_kernel,
        [shape((4, 32, N), BF), shape((3, 4, 32, N), F32)],
        [VMEM, VMEM, ANY],
        [ANY, ANY],
        [vm((3, 4, 32, N), F32), vm((3, 4, 32, N), F32), vm((4, 32, N), BF), pltpu.SemaphoreType.DMA((7,))],
    )(home.reshape(64, 40, 128), bf(unpack_rows()), velocity)


def solution(mesh):
    in_specs = (
        P("pencil", "start", None),
        P("pencil", "start", None),
        P("start", "pencil", None, None),
        P("start", "pencil"),
        P("start", "pencil"),
        P("start", "pencil"),
    )
    out_specs = (P("pencil", "start", None), P("start", "pencil", None, None))
    return jax.shard_map(local, mesh=mesh, in_specs=in_specs, out_specs=out_specs, check_vma=False)
```

```python
import math

import jax
import jax.numpy as jnp
import numpy as np
from jax import lax
from jax.experimental import pallas as pl
from jax.experimental.pallas import tpu as pltpu
from jax.sharding import PartitionSpec as P

Q = 16
N = 512
H1_WEIGHT = 64.0
FORCE_GAIN = 32.0
BF = jnp.bfloat16
F32 = jnp.float32
NN = ((1,), (0,))
NT = ((1,), (1,))


def wave_numbers():
    k = np.arange(N)
    signed = np.where(k < N // 2, k, k - N)
    signed = np.where(k == N // 2, 0, signed)
    return signed * (2.0 * math.pi / N)


def derivative_matrix():
    k = np.arange(N)
    lag = np.arange(N)
    row = (np.sin(2.0 * math.pi * ((k[:, None] * lag[None, :]) % N) / N) * wave_numbers()[:, None]).sum(0) / N
    return row[(lag[None, :] - lag[:, None]) % N]


def modes():
    return np.concatenate([np.arange(N // 2 + 1), np.arange(1, N // 2)])


def basis(points):
    angle = 2.0 * math.pi * ((modes()[:, None] * points[None, :]) % N) / N
    is_cos = (np.arange(N) <= N // 2)[:, None]
    return np.where(is_cos, np.cos(angle), np.sin(angle))


def pack_rows():
    pick = np.zeros((32, 6, 4, 384), np.float32)
    for z in range(32):
        other = (z + (1 if z % 2 else -1)) % 32
        for x in range(4):
            pick[z, 0, x, x * 32 + z] = 1
            pick[z, 1, x, x * 32 + (z ^ 1)] = 1
            pick[z, 2, x, x * 32 + other] = 1
            pick[z, 3, x, 128 + x * 32 + z] = 1
            pick[z, 4, x, 256 + z * 4 + x] = 1
            pick[z, 5, x, 256 + z * 4 + x] = 1
    return pick.reshape(768, 384)


def unpack_rows():
    r = np.arange(N)
    role, x, z = r // 128, (r // 32) % 4, r % 32
    device = (z // 2) * 8 + (role // 2) * 4 + (z % 2) * 2 + role % 2
    pick = np.zeros((N, N), np.float32)
    pick[r, (np.array(PLACE)[device // 2] * 2 + device % 2) * 4 + x] = 1
    return pick


PAIRS = [int(i) for i in np.random.RandomState(3).permutation(64)]
PLACE = [PAIRS.index(i) for i in range(64)]
ORDER = [2 * i + j for i in PAIRS for j in (0, 1)]

PARTNER = (0, 1, 4, 5)


def quarter_of(device):
    return ((device >> 1) & 2) + (device & 1)


def bf(x):
    return jnp.asarray(np.asarray(x, np.float32), BF)


def dot(a, b, dims=NN):
    return lax.dot_general(a, b, (dims, ((), ())), preferred_element_type=F32)


def iota(shape, axis):
    return lax.broadcasted_iota(jnp.int32, shape, axis)


def cubic(level):
    t = (level + 0.5) / Q
    return [
        -t * (t - 1.0) * (t - 2.0) / 6.0,
        (t + 1.0) * (t - 1.0) * (t - 2.0) / 2.0,
        -(t + 1.0) * t * (t - 2.0) / 2.0,
        (t + 1.0) * t * (t - 1.0) / 6.0,
    ]


def mode_waves(shape, axis):
    i = iota(shape, axis)
    k = jnp.where(i < N // 2, i, i - N // 2)
    wave = k.astype(F32) * (2.0 * math.pi / N)
    return wave, jnp.where(k == 0, 1.0, 2.0)


def fetch(refs, scratch, sem):
    copies = [pltpu.make_async_copy(r, v, sem.at[i]) for i, (r, v) in enumerate(zip(refs, scratch))]
    for copy in copies:
        copy.start()
    return copies


def pack_kernel(owner_ref, offset_ref, weight_ref, template_ref, image_ref, pick_ref, out_ref, owner, offset, weight, template, image, pick, sem):
    copies = fetch(
        (owner_ref, offset_ref, weight_ref, template_ref, image_ref, pick_ref),
        (owner, offset, weight, template, image, pick),
        sem,
    )
    me = lax.axis_index("pencil")
    for copy in copies[:3]:
        copy.wait()
    move = ((owner[...] - me + 130) & 127) - 2
    rel = (move * 4 + (offset[...] >> 6)).astype(F32)
    level = weight[...].astype(F32)
    taps = cubic(level)
    items = [rel]
    for tap in taps:
        items.append(tap.astype(BF).astype(F32))
    for tap, high in zip(taps, items[1:5]):
        items.append(tap - high)
    row = iota((32, 256), 0)
    value = jnp.zeros((32, 256), F32)
    for section in range(2):
        for i, item in enumerate(items):
            value = jnp.where(row == 16 * section + i, item[section : section + 1], value)
    blank = jnp.zeros((32, 256), F32)
    codes = jnp.concatenate(
        [
            jnp.concatenate([value, blank, blank, blank], axis=0),
            jnp.concatenate([blank, value, blank, blank], axis=0),
        ],
        axis=1,
    ).astype(BF)
    row, col = iota((N, 256), 0), iota((N, 256), 1)
    q, z, x = row >> 7, (row >> 2) & 31, row & 3
    other = (z + 2 * (z & 1) - 1) & 31
    near = jnp.where(col == x * 64 + (z >> 1) * 4 + q, 1.0, 0.0)
    far = jnp.where(col == x * 64 + (other >> 1) * 4 + q, 1.0, 0.0)
    codes = dot(jnp.concatenate([near, far], axis=1).astype(BF), codes, NT).astype(BF)
    codes = jnp.concatenate([codes[128 * i : 128 * i + 128] for i in range(4)], axis=1)
    for copy in copies[3:]:
        copy.wait()
    stack = jnp.concatenate([template[...].reshape(128, N), image[...].reshape(128, N), codes], axis=0)
    rows = dot(pick[...], stack)
    low = iota((32, 8, 128), 1) < 4
    for pair in range(2):
        units = []
        for q in (2 * pair, 2 * pair + 1):
            part = rows[:, 128 * q : 128 * q + 128].reshape(32, 3, 8, 128)
            units += [part[:, 0], part[:, 1], part[:, 2]]
        a, b, c, d, e, f = units
        d, e = pltpu.roll(d, 4, 1), pltpu.roll(e, 4, 1)
        tiles = [a, b, jnp.where(low, c, d), jnp.where(low, d, e), jnp.where(low, e, f)]
        tiles = jnp.concatenate(tiles, axis=1).astype(BF)
        for z in range(32):
            out_ref[PLACE[(z // 2) * 4 + pair * 2 + z % 2]] = tiles[z]


def units_of(ref, places=None):
    t = [ref[:, 8 * i : 8 * i + 8, :].astype(F32) for i in range(5)]
    if places is not None:
        t = [jnp.concatenate([v[i : i + 1] for i in places], axis=0) for v in t]
    low = iota((64, 8, 128), 1) < 4
    units = [
        jnp.where(low, t[0], t[2]),
        pltpu.roll(jnp.where(low, t[3], t[0]), 4, 1),
        jnp.where(low, t[1], t[3]),
        pltpu.roll(jnp.where(low, t[4], t[1]), 4, 1),
        jnp.where(low, t[2], t[4]),
    ]
    return [u.reshape(N, 128) for u in units]


def units_to(ref, units):
    a, b, c, d, e = [u.reshape(64, 8, 128) for u in units]
    low = iota((64, 8, 128), 1) < 4
    turned_b, turned_d = pltpu.roll(b, 4, 1), pltpu.roll(d, 4, 1)
    tiles = [
        jnp.where(low, a, turned_b),
        jnp.where(low, c, turned_d),
        jnp.where(low, e, a),
        jnp.where(low, turned_b, c),
        jnp.where(low, turned_d, e),
    ]
    tiles = jnp.concatenate(tiles, axis=1).astype(BF)
    for i in range(64):
        ref[PLACE[i]] = tiles[i]


def transport(codes, at, f):
    taps = []
    for i in range(4):
        part = codes[128 * i : 128 * i + 128]
        rel = part[:, at : at + 1]
        pieces = [[part[:, at + j + k : at + j + 1 + k] for k in range(4)] for j in (1, 5)]
        moved = []
        for tile, first, count in ((0, 0, 128), (-1, 0, 16), (1, 112, 16)):
            rows = slice(first, first + count)
            row = iota((count, 128), 0) + first
            lag = (iota((count, 128), 1) + 128 * tile - (row & -4)).astype(F32) - rel[rows]
            band = []
            for piece in pieces:
                weight = jnp.zeros((count, 128), F32)
                for k in range(4):
                    weight = jnp.where(lag == k, piece[k][rows], weight)
                band.append(weight.astype(BF))
            j = (i + tile) % 4
            source = f[128 * j : 128 * j + 128]
            moved.append(dot(jnp.concatenate(band, axis=1), jnp.concatenate([source, source], axis=0)))
        mid, down, up = moved
        taps += [mid[:16] + down, mid[16:112], mid[112:] + up]
    return jnp.concatenate(taps, axis=0).astype(BF)


def transport_kernel(got_ref, deriv_ref, out0_ref, out1_ref, out2_ref, out3_ref, warped_ref, pieces):
    me = lax.axis_index("pencil")
    own, partner, other, image, codes = units_of(got_ref, PLACE)
    near = jnp.concatenate([own, partner], axis=1).astype(BF)
    other = other.astype(BF)
    for section in range(2):
        near = transport(codes, 16 * section, near)
        other = transport(codes, 32 + 16 * section, other)
    warped = near[:, :128]
    residual = image - warped.astype(F32)
    image = image.astype(BF)
    sign = jnp.where((me & 2) == 0, 0.5, -0.5).astype(F32)
    slope_z = (near[:, 128:].astype(F32) - other.astype(F32)) * sign
    warped_ref[...] = warped
    pieces[0] = (residual * dot(deriv_ref[...], warped)).astype(BF)
    pieces[1, 0:256] = warped[0:256]
    pieces[1, 256:512] = image[0:256]
    pieces[2] = (residual * slope_z).astype(BF)
    pieces[3, 0:256] = warped[256:512]
    pieces[3, 256:512] = image[256:512]
    for s, ref in enumerate((out0_ref, out1_ref, out2_ref, out3_ref)):
        ref[...] = pieces[quarter_of(me) ^ s]


def smooth_kernel(p0_ref, p1_ref, p2_ref, p3_ref, warped_ref, deriv_ref, table_ref, flip_ref, out_ref, plane):
    role = quarter_of(lax.axis_index("pencil"))
    for s, ref in enumerate((p0_ref, p1_ref, p2_ref, p3_ref)):
        plane[:, pl.ds(pl.multiple_of((role ^ s) * 128, 128), 128)] = ref[...]

    @pl.when((role & 1) == 1)
    def _():
        half = plane[0:256]
        slope_y = -dot(half, deriv_ref[...])
        force = ((plane[256:512].astype(F32) - half.astype(F32)) * slope_y).astype(BF)
        at = (role >> 1) * 256
        plane[pl.ds(pl.multiple_of(at, 256), 256)] = force
        plane[pl.ds(pl.multiple_of(256 - at, 256), 256)] = jnp.zeros((256, N), BF)

    spec = dot(plane[...], flip_ref[...]).astype(BF)
    wave_x, scale_x = mode_waves((N, 1), 0)
    wave_y, scale_y = mode_waves((1, N), 1)
    gain = (scale_x * scale_y * (FORCE_GAIN / (N * N))) / (1.0 + H1_WEIGHT * (wave_x * wave_x + wave_y * wave_y))
    bent = (dot(table_ref[...], spec) * gain).astype(BF)
    back = dot(flip_ref[...], bent).astype(BF)
    smooth = dot(back, table_ref[...])
    units = [smooth[:, 128 * s : 128 * s + 128] for s in range(4)]
    units_to(out_ref, units + [warped_ref[...].astype(F32)])


def finish_kernel(home_ref, pick_ref, velocity_ref, out_warped_ref, out_ref, velocity, result, warped, sem):
    loads = fetch([velocity_ref.at[c] for c in range(3)], [velocity.at[c] for c in range(3)], sem)
    pick = pick_ref[...]
    units = units_of(home_ref)
    rows = jnp.concatenate(units[:4], axis=1).astype(BF)
    turned = dot(pick, units[4].astype(BF))
    for r in range(4):
        warped[:, :, 128 * r : 128 * r + 128] = turned[128 * r : 128 * r + 128].reshape(4, 32, 128).astype(BF)
    stores = [pltpu.make_async_copy(warped, out_warped_ref, sem.at[3])]
    stores[0].start()
    for c in range(3):
        which = pick[128 * c : 128 * c + 128]
        if c == 1:
            which = which + pick[384:512]
        part = dot(which, rows).reshape(4, 32, N)
        loads[c].wait()
        result[c] = velocity[c] + part
        store = pltpu.make_async_copy(result.at[c], out_ref.at[c], sem.at[4 + c])
        store.start()
        stores.append(store)
    for store in stores:
        store.wait()


ANY = pl.BlockSpec(memory_space=pltpu.HBM)
VMEM = pl.BlockSpec(memory_space=pltpu.VMEM)


def call(kernel, outs, in_specs, out_specs, scratch, grant=48 << 20):
    return pl.pallas_call(
        kernel,
        out_shape=outs,
        in_specs=in_specs,
        out_specs=out_specs,
        scratch_shapes=scratch,
        compiler_params=pltpu.CompilerParams(vmem_limit_bytes=grant),
    )


def swap(chunks):
    chunks = chunks.reshape(640, 4, 128)
    chunks = lax.all_to_all(chunks, "pencil", 0, 0, axis_index_groups=[ORDER], tiled=True)
    return chunks.reshape(64, 40, 128)


def local(template, reference_image, velocity, dep_owner, dep_offset, dep_weight):
    shape = jax.ShapeDtypeStruct
    piece = shape((N, 128), BF)
    vm = pltpu.VMEM

    pick = bf(pack_rows())
    inputs = (dep_owner, dep_offset, dep_weight, template, reference_image, pick)
    pack = call(
        pack_kernel,
        shape((64, 40, 128), BF),
        [ANY] * 6,
        VMEM,
        [vm(a.shape, a.dtype) for a in inputs] + [pltpu.SemaphoreType.DMA((6,))],
        65000000,
    )(*inputs)
    got = swap(pack)

    deriv = bf(derivative_matrix())
    *parts, warped = call(
        transport_kernel,
        [piece] * 5,
        [VMEM] * 2,
        [VMEM] * 5,
        [vm((4, N, 128), BF)],
    )(got, deriv)
    for s in (1, 2, 3):
        parts[s] = lax.ppermute(parts[s], "pencil", [(i ^ PARTNER[s], i) for i in range(128)])

    table = basis(np.arange(N))
    send = call(
        smooth_kernel,
        shape((64, 40, 128), BF),
        [VMEM] * 8,
        VMEM,
        [vm((N, N), BF)],
    )(*parts, warped, deriv, bf(table), bf(table.T))
    home = swap(send)

    return call(
        finish_kernel,
        [shape((4, 32, N), BF), shape((3, 4, 32, N), F32)],
        [VMEM, VMEM, ANY],
        [ANY, ANY],
        [vm((3, 4, 32, N), F32), vm((3, 4, 32, N), F32), vm((4, 32, N), BF), pltpu.SemaphoreType.DMA((7,))],
    )(home, bf(unpack_rows()), velocity)


def solution(mesh):
    in_specs = (
        P("pencil", "start", None),
        P("pencil", "start", None),
        P("start", "pencil", None, None),
        P("start", "pencil"),
        P("start", "pencil"),
        P("start", "pencil"),
    )
    out_specs = (P("pencil", "start", None), P("start", "pencil", None, None))
    return jax.shard_map(local, mesh=mesh, in_specs=in_specs, out_specs=out_specs, check_vma=False)
```

```python
import math

import jax
import jax.numpy as jnp
import numpy as np
from jax import lax
from jax.experimental import pallas as pl
from jax.experimental.pallas import tpu as pltpu
from jax.sharding import PartitionSpec as P

Q = 16
N = 512
H1_WEIGHT = 64.0
FORCE_GAIN = 32.0
BF = jnp.bfloat16
F32 = jnp.float32
NN = ((1,), (0,))
NT = ((1,), (1,))


def wave_numbers():
    k = np.arange(N)
    signed = np.where(k < N // 2, k, k - N)
    signed = np.where(k == N // 2, 0, signed)
    return signed * (2.0 * math.pi / N)


def derivative_matrix():
    k = np.arange(N)
    lag = np.arange(N)
    row = (np.sin(2.0 * math.pi * ((k[:, None] * lag[None, :]) % N) / N) * wave_numbers()[:, None]).sum(0) / N
    return row[(lag[None, :] - lag[:, None]) % N]


def modes():
    return np.concatenate([np.arange(N // 2 + 1), np.arange(1, N // 2)])


def basis(points):
    angle = 2.0 * math.pi * ((modes()[:, None] * points[None, :]) % N) / N
    is_cos = (np.arange(N) <= N // 2)[:, None]
    return np.where(is_cos, np.cos(angle), np.sin(angle))


def pack_rows():
    pick = np.zeros((32, 24, 320), np.float32)
    for z in range(32):
        other = (z + (1 if z % 2 else -1)) % 32
        for x in range(4):
            pick[z, x, x * 32 + z] = 1
            pick[z, 4 + x, x * 32 + (z ^ 1)] = 1
            pick[z, 8 + x, x * 32 + other] = 1
            pick[z, 12 + x, 128 + x * 32 + z] = 1
        pick[z, 16, 256 + z * 2] = 1
        pick[z, 17, 257 + z * 2] = 1
    return pick.reshape(768, 320)


def unpack_rows():
    r = np.arange(N)
    role, x, z = r // 128, (r // 32) % 4, r % 32
    device = (z // 2) * 8 + (role // 2) * 4 + (z % 2) * 2 + role % 2
    pick = np.zeros((N, N), np.float32)
    pick[r, (np.array(PLACE)[device // 2] * 2 + device % 2) * 4 + x] = 1
    return pick


QUADS = [int(i) for i in np.random.RandomState(1).permutation(32)]
PAIRS = [2 * i + j for i in QUADS for j in (0, 1)]
ORDER = [4 * i + j for i in QUADS for j in range(4)]
QUAD_PLACE = [QUADS.index(i) for i in range(32)]
PLACE = [PAIRS.index(i) for i in range(64)]

PARTNER = (0, 1, 4, 5)


def quarter_of(device):
    return ((device >> 1) & 2) + (device & 1)


def bf(x):
    return jnp.asarray(np.asarray(x, np.float32), BF)


def dot(a, b, dims=NN):
    return lax.dot_general(a, b, (dims, ((), ())), preferred_element_type=F32)


def iota(shape, axis):
    return lax.broadcasted_iota(jnp.int32, shape, axis)


def cubic(level):
    t = (level + 0.5) / Q
    return [
        -t * (t - 1.0) * (t - 2.0) / 6.0,
        (t + 1.0) * (t - 1.0) * (t - 2.0) / 2.0,
        -(t + 1.0) * t * (t - 2.0) / 2.0,
        (t + 1.0) * t * (t - 1.0) / 6.0,
    ]


def mode_waves(shape, axis):
    i = iota(shape, axis)
    k = jnp.where(i < N // 2, i, i - N // 2)
    wave = k.astype(F32) * (2.0 * math.pi / N)
    return wave, jnp.where(k == 0, 1.0, 2.0)


def fetch(refs, scratch, sem):
    copies = [pltpu.make_async_copy(r, v, sem.at[i]) for i, (r, v) in enumerate(zip(refs, scratch))]
    for copy in copies:
        copy.start()
    return copies


def pack_kernel(owner_ref, offset_ref, weight_ref, template_ref, image_ref, pick_ref, out_ref, owner, offset, weight, template, image, pick, sem):
    copies = fetch(
        (owner_ref, offset_ref, weight_ref, template_ref, image_ref, pick_ref),
        (owner, offset, weight, template, image, pick),
        sem,
    )
    me = lax.axis_index("pencil")
    for copy in copies[:3]:
        copy.wait()
    move = ((owner[...] - me + 130) & 127) - 2
    rel = (move * 4 + (offset[...] >> 6)).astype(F32)
    level = weight[...].astype(F32)
    taps = cubic(level)
    items = [rel]
    for tap in taps:
        items.append(tap.astype(BF).astype(F32))
    for tap, high in zip(taps, items[1:5]):
        items.append(tap - high)
    row = iota((32, 256), 0)
    value = jnp.zeros((32, 256), F32)
    for section in range(2):
        for i, item in enumerate(items):
            value = jnp.where(row == 16 * section + i, item[section : section + 1], value)
    blank = jnp.zeros((32, 256), F32)
    codes = jnp.concatenate(
        [jnp.concatenate([value if i == j else blank for j in range(4)], axis=1) for i in range(4)], axis=0
    ).astype(BF)
    row, col = iota((256, 256), 0), iota((256, 256), 1)
    q, z = row >> 6, (row >> 1) & 31
    other = (z + 2 * (z & 1) - 1) & 31
    hot = [
        jnp.where(col == (2 * (row & 1) + x) * 64 + (plane >> 1) * 4 + q, 1.0, 0.0)
        for x in range(2)
        for plane in (z, other)
    ]
    codes = dot(jnp.concatenate(hot, axis=1).astype(BF), codes, NT).astype(BF)
    codes = jnp.concatenate([codes[64 * i : 64 * i + 64] for i in range(4)], axis=1)
    for copy in copies[3:]:
        copy.wait()
    stack = jnp.concatenate([template[...].reshape(128, N), image[...].reshape(128, N), codes], axis=0)
    rows = dot(pick[...], stack)
    at = iota((16, 8, 128), 1)
    for half in range(2):
        chunks = []
        for j in range(4):
            q = 2 * half + (j & 1)
            part = rows[:, 128 * q : 128 * q + 128].reshape(16, 2, 3, 8, 128)[:, j >> 1]
            part = [part[:, i] for i in range(3)]
            chunks.append([pltpu.roll(v, 2 * j, 1) for v in part] if j else part)
        (a0, b0, c0), (a1, b1, c1), (a2, b2, c2), (a3, b3, c3) = chunks
        tiles = [
            a0,
            b0,
            jnp.where(at < 2, c0, a1),
            jnp.where(at < 2, a1, b1),
            jnp.where(at < 2, b1, jnp.where(at < 4, c1, a2)),
            jnp.where(at < 4, a2, b2),
            jnp.where(at < 4, b2, jnp.where(at < 6, c2, a3)),
            jnp.where(at < 6, a3, b3),
            jnp.where(at < 6, b3, c3),
        ]
        tiles = jnp.concatenate(tiles, axis=1).astype(BF)
        for z in range(16):
            out_ref[QUAD_PLACE[2 * z + half]] = tiles[z]


def planes_of(ref):
    t = [ref[:, 8 * i : 8 * i + 8, :].astype(F32) for i in range(9)]
    t = [jnp.concatenate([v[i : i + 1] for i in QUAD_PLACE], axis=0) for v in t]
    at = iota((32, 8, 128), 1)
    low = at < 4

    def turn(v, by):
        return pltpu.roll(v, by, 1)

    def join(first, second):
        return jnp.stack([first, second], axis=1).reshape(N, 128)

    units = []
    for i in range(2):
        v0 = t[i]
        v1 = jnp.where(at < 2, t[3 + i], t[2 + i])
        v2 = jnp.where(low, t[5 + i], t[4 + i])
        v3 = jnp.where(at < 6, t[7 + i], t[6 + i])
        units.append(join(jnp.where(low, v0, turn(v1, 2)), jnp.where(low, turn(v2, 4), turn(v3, 6))))
        units.append(join(jnp.where(low, turn(v0, 4), turn(v1, 6)), jnp.where(low, v2, turn(v3, 2))))
    codes = []
    for v in (jnp.where(low, t[2], turn(t[4], 2)), jnp.where(low, turn(t[6], 4), turn(t[8], 6))):
        v = jnp.where((at & 3) == 0, v, jnp.where((at & 3) == 3, turn(v, 2), turn(v, 1)))
        codes.append(jnp.where((at & 1) == 1, pltpu.roll(v, 64, 2), v))
    return units + [join(*codes)]


def units_of(ref):
    t = [ref[:, 8 * i : 8 * i + 8, :].astype(F32) for i in range(5)]
    low = iota((64, 8, 128), 1) < 4
    units = [
        jnp.where(low, t[0], t[2]),
        pltpu.roll(jnp.where(low, t[3], t[0]), 4, 1),
        jnp.where(low, t[1], t[3]),
        pltpu.roll(jnp.where(low, t[4], t[1]), 4, 1),
        jnp.where(low, t[2], t[4]),
    ]
    return [u.reshape(N, 128) for u in units]


def units_to(ref, units):
    a, b, c, d, e = [u.reshape(64, 8, 128) for u in units]
    low = iota((64, 8, 128), 1) < 4
    turned_b, turned_d = pltpu.roll(b, 4, 1), pltpu.roll(d, 4, 1)
    tiles = [
        jnp.where(low, a, turned_b),
        jnp.where(low, c, turned_d),
        jnp.where(low, e, a),
        jnp.where(low, turned_b, c),
        jnp.where(low, turned_d, e),
    ]
    tiles = jnp.concatenate(tiles, axis=1).astype(BF)
    for i in range(64):
        ref[PLACE[i]] = tiles[i]


def transport(codes, at, f):
    taps = []
    for i in range(4):
        part = codes[128 * i : 128 * i + 128]
        rel = part[:, at : at + 1]
        pieces = [[part[:, at + j + k : at + j + 1 + k] for k in range(4)] for j in (1, 5)]
        moved = []
        for tile, first, count in ((0, 0, 128), (-1, 0, 16), (1, 112, 16)):
            rows = slice(first, first + count)
            row = iota((count, 128), 0) + first
            lag = (iota((count, 128), 1) + 128 * tile - (row & -4)).astype(F32) - rel[rows]
            band = []
            for piece in pieces:
                weight = jnp.zeros((count, 128), F32)
                for k in range(4):
                    weight = jnp.where(lag == k, piece[k][rows], weight)
                band.append(weight.astype(BF))
            j = (i + tile) % 4
            source = f[128 * j : 128 * j + 128]
            moved.append(dot(jnp.concatenate(band, axis=1), jnp.concatenate([source, source], axis=0)))
        mid, down, up = moved
        taps += [mid[:16] + down, mid[16:112], mid[112:] + up]
    return jnp.concatenate(taps, axis=0).astype(BF)


def transport_kernel(got_ref, deriv_ref, out0_ref, out1_ref, out2_ref, out3_ref, warped_ref, pieces):
    me = lax.axis_index("pencil")
    own, partner, other, image, codes = planes_of(got_ref)
    near = jnp.concatenate([own, partner], axis=1).astype(BF)
    other = other.astype(BF)
    for section in range(2):
        near = transport(codes, 16 * section, near)
        other = transport(codes, 32 + 16 * section, other)
    warped = near[:, :128]
    residual = image - warped.astype(F32)
    image = image.astype(BF)
    sign = jnp.where((me & 2) == 0, 0.5, -0.5).astype(F32)
    slope_z = (near[:, 128:].astype(F32) - other.astype(F32)) * sign
    warped_ref[...] = warped
    pieces[0] = (residual * dot(deriv_ref[...], warped)).astype(BF)
    pieces[1, 0:256] = warped[0:256]
    pieces[1, 256:512] = image[0:256]
    pieces[2] = (residual * slope_z).astype(BF)
    pieces[3, 0:256] = warped[256:512]
    pieces[3, 256:512] = image[256:512]
    for s, ref in enumerate((out0_ref, out1_ref, out2_ref, out3_ref)):
        ref[...] = pieces[quarter_of(me) ^ s]


def smooth_kernel(p0_ref, p1_ref, p2_ref, p3_ref, warped_ref, deriv_ref, table_ref, flip_ref, out_ref, plane):
    role = quarter_of(lax.axis_index("pencil"))
    for s, ref in enumerate((p0_ref, p1_ref, p2_ref, p3_ref)):
        plane[:, pl.ds(pl.multiple_of((role ^ s) * 128, 128), 128)] = ref[...]

    @pl.when((role & 1) == 1)
    def _():
        half = plane[0:256]
        slope_y = -dot(half, deriv_ref[...])
        force = ((plane[256:512].astype(F32) - half.astype(F32)) * slope_y).astype(BF)
        at = (role >> 1) * 256
        plane[pl.ds(pl.multiple_of(at, 256), 256)] = force
        plane[pl.ds(pl.multiple_of(256 - at, 256), 256)] = jnp.zeros((256, N), BF)

    spec = dot(plane[...], flip_ref[...]).astype(BF)
    wave_x, scale_x = mode_waves((N, 1), 0)
    wave_y, scale_y = mode_waves((1, N), 1)
    gain = (scale_x * scale_y * (FORCE_GAIN / (N * N))) / (1.0 + H1_WEIGHT * (wave_x * wave_x + wave_y * wave_y))
    bent = (dot(table_ref[...], spec) * gain).astype(BF)
    back = dot(flip_ref[...], bent).astype(BF)
    smooth = dot(back, table_ref[...])
    units = [smooth[:, 128 * s : 128 * s + 128] for s in range(4)]
    units_to(out_ref, units + [warped_ref[...].astype(F32)])


def finish_kernel(home_ref, pick_ref, velocity_ref, out_warped_ref, out_ref, velocity, result, warped, sem):
    loads = fetch([velocity_ref.at[c] for c in range(3)], [velocity.at[c] for c in range(3)], sem)
    pick = pick_ref[...]
    units = units_of(home_ref)
    rows = jnp.concatenate(units[:4], axis=1).astype(BF)
    turned = dot(pick, units[4].astype(BF))
    for r in range(4):
        warped[:, :, 128 * r : 128 * r + 128] = turned[128 * r : 128 * r + 128].reshape(4, 32, 128).astype(BF)
    stores = [pltpu.make_async_copy(warped, out_warped_ref, sem.at[3])]
    stores[0].start()
    for c in range(3):
        which = pick[128 * c : 128 * c + 128]
        if c == 1:
            which = which + pick[384:512]
        part = dot(which, rows).reshape(4, 32, N)
        loads[c].wait()
        result[c] = velocity[c] + part
        store = pltpu.make_async_copy(result.at[c], out_ref.at[c], sem.at[4 + c])
        store.start()
        stores.append(store)
    for store in stores:
        store.wait()


ANY = pl.BlockSpec(memory_space=pltpu.HBM)
VMEM = pl.BlockSpec(memory_space=pltpu.VMEM)


def call(kernel, outs, in_specs, out_specs, scratch, grant=48 << 20):
    return pl.pallas_call(
        kernel,
        out_shape=outs,
        in_specs=in_specs,
        out_specs=out_specs,
        scratch_shapes=scratch,
        compiler_params=pltpu.CompilerParams(vmem_limit_bytes=grant),
    )


def swap(chunks, rows):
    chunks_of = chunks.reshape(-1, rows, 128)
    chunks_of = lax.all_to_all(chunks_of, "pencil", 0, 0, axis_index_groups=[ORDER], tiled=True)
    return chunks_of.reshape(chunks.shape)


def local(template, reference_image, velocity, dep_owner, dep_offset, dep_weight):
    shape = jax.ShapeDtypeStruct
    piece = shape((N, 128), BF)
    vm = pltpu.VMEM

    pick = bf(pack_rows())
    inputs = (dep_owner, dep_offset, dep_weight, template, reference_image, pick)
    pack = call(
        pack_kernel,
        shape((32, 72, 128), BF),
        [ANY] * 6,
        VMEM,
        [vm(a.shape, a.dtype) for a in inputs] + [pltpu.SemaphoreType.DMA((6,))],
        65000000,
    )(*inputs)
    got = swap(pack, 2)

    deriv = bf(derivative_matrix())
    *parts, warped = call(
        transport_kernel,
        [piece] * 5,
        [VMEM] * 2,
        [VMEM] * 5,
        [vm((4, N, 128), BF)],
    )(got, deriv)
    for s in (1, 2, 3):
        parts[s] = lax.ppermute(parts[s], "pencil", [(i ^ PARTNER[s], i) for i in range(128)])

    table = basis(np.arange(N))
    send = call(
        smooth_kernel,
        shape((64, 40, 128), BF),
        [VMEM] * 8,
        VMEM,
        [vm((N, N), BF)],
    )(*parts, warped, deriv, bf(table), bf(table.T))
    home = swap(send, 4)

    return call(
        finish_kernel,
        [shape((4, 32, N), BF), shape((3, 4, 32, N), F32)],
        [VMEM, VMEM, ANY],
        [ANY, ANY],
        [vm((3, 4, 32, N), F32), vm((3, 4, 32, N), F32), vm((4, 32, N), BF), pltpu.SemaphoreType.DMA((7,))],
    )(home, bf(unpack_rows()), velocity)


def solution(mesh):
    in_specs = (
        P("pencil", "start", None),
        P("pencil", "start", None),
        P("start", "pencil", None, None),
        P("start", "pencil"),
        P("start", "pencil"),
        P("start", "pencil"),
    )
    out_specs = (P("pencil", "start", None), P("start", "pencil", None, None))
    return jax.shard_map(local, mesh=mesh, in_specs=in_specs, out_specs=out_specs, check_vma=False)
```

```python
import math

import jax
import jax.numpy as jnp
import numpy as np
from jax import lax
from jax.experimental import pallas as pl
from jax.experimental.pallas import tpu as pltpu
from jax.sharding import PartitionSpec as P

Q = 16
N = 512
H1_WEIGHT = 64.0
FORCE_GAIN = 32.0
BF = jnp.bfloat16
F32 = jnp.float32
NN = ((1,), (0,))
NT = ((1,), (1,))


def wave_numbers():
    k = np.arange(N)
    signed = np.where(k < N // 2, k, k - N)
    signed = np.where(k == N // 2, 0, signed)
    return signed * (2.0 * math.pi / N)


def derivative_matrix():
    k = np.arange(N)
    lag = np.arange(N)
    row = (np.sin(2.0 * math.pi * ((k[:, None] * lag[None, :]) % N) / N) * wave_numbers()[:, None]).sum(0) / N
    return row[(lag[None, :] - lag[:, None]) % N]


def modes():
    return np.concatenate([np.arange(N // 2 + 1), np.arange(1, N // 2)])


def basis(points):
    angle = 2.0 * math.pi * ((modes()[:, None] * points[None, :]) % N) / N
    is_cos = (np.arange(N) <= N // 2)[:, None]
    return np.where(is_cos, np.cos(angle), np.sin(angle))


def pack_rows():
    pick = np.zeros((32, 24, 320), np.float32)
    for z in range(32):
        other = (z + (1 if z % 2 else -1)) % 32
        for x in range(4):
            pick[z, x, x * 32 + z] = 1
            pick[z, 4 + x, x * 32 + (z ^ 1)] = 1
            pick[z, 8 + x, x * 32 + other] = 1
            pick[z, 12 + x, 128 + x * 32 + z] = 1
        pick[z, 16, 256 + z * 2] = 1
        pick[z, 17, 257 + z * 2] = 1
    return pick.reshape(768, 320)


def unpack_rows():
    r = np.arange(N)
    role, x, z = r // 128, (r // 32) % 4, r % 32
    device = (z // 2) * 8 + (role // 2) * 4 + (z % 2) * 2 + role % 2
    pick = np.zeros((N, N), np.float32)
    pick[r, (np.array(PLACE)[device // 2] * 2 + device % 2) * 4 + x] = 1
    return pick


QUADS = [int(i) for i in np.random.RandomState(1).permutation(32)]
PAIRS = [int(i) for i in np.random.RandomState(24).permutation(64)]
ORDERS = [[4 * i + j for i in QUADS for j in range(4)], [2 * i + j for i in PAIRS for j in (0, 1)]]
QUAD_PLACE = [QUADS.index(i) for i in range(32)]
PLACE = [PAIRS.index(i) for i in range(64)]

PARTNER = (0, 1, 4, 5)


def quarter_of(device):
    return ((device >> 1) & 2) + (device & 1)


def bf(x):
    return jnp.asarray(np.asarray(x, np.float32), BF)


def dot(a, b, dims=NN):
    return lax.dot_general(a, b, (dims, ((), ())), preferred_element_type=F32)


def iota(shape, axis):
    return lax.broadcasted_iota(jnp.int32, shape, axis)


def cubic(level):
    t = (level + 0.5) / Q
    return [
        -t * (t - 1.0) * (t - 2.0) / 6.0,
        (t + 1.0) * (t - 1.0) * (t - 2.0) / 2.0,
        -(t + 1.0) * t * (t - 2.0) / 2.0,
        (t + 1.0) * t * (t - 1.0) / 6.0,
    ]


def mode_waves(shape, axis):
    i = iota(shape, axis)
    k = jnp.where(i < N // 2, i, i - N // 2)
    wave = k.astype(F32) * (2.0 * math.pi / N)
    return wave, jnp.where(k == 0, 1.0, 2.0)


def fetch(refs, scratch, sem):
    copies = [pltpu.make_async_copy(r, v, sem.at[i]) for i, (r, v) in enumerate(zip(refs, scratch))]
    for copy in copies:
        copy.start()
    return copies


def pack_kernel(owner_ref, offset_ref, weight_ref, template_ref, image_ref, pick_ref, out_ref, owner, offset, weight, template, image, pick, sem):
    copies = fetch(
        (owner_ref, offset_ref, weight_ref, template_ref, image_ref, pick_ref),
        (owner, offset, weight, template, image, pick),
        sem,
    )
    me = lax.axis_index("pencil")
    for copy in copies[:3]:
        copy.wait()
    move = ((owner[...] - me + 130) & 127) - 2
    rel = (move * 4 + (offset[...] >> 6)).astype(F32)
    level = weight[...].astype(F32)
    taps = cubic(level)
    items = [rel]
    for tap in taps:
        items.append(tap.astype(BF).astype(F32))
    for tap, high in zip(taps, items[1:5]):
        items.append(tap - high)
    row = iota((32, 256), 0)
    value = jnp.zeros((32, 256), F32)
    for section in range(2):
        for i, item in enumerate(items):
            value = jnp.where(row == 16 * section + i, item[section : section + 1], value)
    blank = jnp.zeros((32, 256), F32)
    codes = jnp.concatenate(
        [jnp.concatenate([value if i == j else blank for j in range(4)], axis=1) for i in range(4)], axis=0
    ).astype(BF)
    row, col = iota((256, 256), 0), iota((256, 256), 1)
    q, z = row >> 6, (row >> 1) & 31
    other = (z + 2 * (z & 1) - 1) & 31
    hot = [
        jnp.where(col == (2 * (row & 1) + x) * 64 + (plane >> 1) * 4 + q, 1.0, 0.0)
        for x in range(2)
        for plane in (z, other)
    ]
    codes = dot(jnp.concatenate(hot, axis=1).astype(BF), codes, NT).astype(BF)
    codes = jnp.concatenate([codes[64 * i : 64 * i + 64] for i in range(4)], axis=1)
    for copy in copies[3:]:
        copy.wait()
    stack = jnp.concatenate([template[...].reshape(128, N), image[...].reshape(128, N), codes], axis=0)
    rows = dot(pick[...], stack)
    at = iota((16, 8, 128), 1)
    for half in range(2):
        chunks = []
        for j in range(4):
            q = 2 * half + (j & 1)
            part = rows[:, 128 * q : 128 * q + 128].reshape(16, 2, 3, 8, 128)[:, j >> 1]
            part = [part[:, i] for i in range(3)]
            chunks.append([pltpu.roll(v, 2 * j, 1) for v in part] if j else part)
        (a0, b0, c0), (a1, b1, c1), (a2, b2, c2), (a3, b3, c3) = chunks
        tiles = [
            a0,
            b0,
            jnp.where(at < 2, c0, a1),
            jnp.where(at < 2, a1, b1),
            jnp.where(at < 2, b1, jnp.where(at < 4, c1, a2)),
            jnp.where(at < 4, a2, b2),
            jnp.where(at < 4, b2, jnp.where(at < 6, c2, a3)),
            jnp.where(at < 6, a3, b3),
            jnp.where(at < 6, b3, c3),
        ]
        tiles = jnp.concatenate(tiles, axis=1).astype(BF)
        for z in range(16):
            out_ref[QUAD_PLACE[2 * z + half]] = tiles[z]


def planes_of(ref):
    t = [ref[:, 8 * i : 8 * i + 8, :].astype(F32) for i in range(9)]
    t = [jnp.concatenate([v[i : i + 1] for i in QUAD_PLACE], axis=0) for v in t]
    at = iota((32, 8, 128), 1)
    low = at < 4

    def turn(v, by):
        return pltpu.roll(v, by, 1)

    def join(first, second):
        return jnp.stack([first, second], axis=1).reshape(N, 128)

    units = []
    for i in range(2):
        v0 = t[i]
        v1 = jnp.where(at < 2, t[3 + i], t[2 + i])
        v2 = jnp.where(low, t[5 + i], t[4 + i])
        v3 = jnp.where(at < 6, t[7 + i], t[6 + i])
        units.append(join(jnp.where(low, v0, turn(v1, 2)), jnp.where(low, turn(v2, 4), turn(v3, 6))))
        units.append(join(jnp.where(low, turn(v0, 4), turn(v1, 6)), jnp.where(low, v2, turn(v3, 2))))
    codes = []
    for v in (jnp.where(low, t[2], turn(t[4], 2)), jnp.where(low, turn(t[6], 4), turn(t[8], 6))):
        v = jnp.where((at & 3) == 0, v, jnp.where((at & 3) == 3, turn(v, 2), turn(v, 1)))
        codes.append(jnp.where((at & 1) == 1, pltpu.roll(v, 64, 2), v))
    return units + [join(*codes)]


def units_of(ref):
    t = [ref[:, 8 * i : 8 * i + 8, :].astype(F32) for i in range(5)]
    low = iota((64, 8, 128), 1) < 4
    units = [
        jnp.where(low, t[0], t[2]),
        pltpu.roll(jnp.where(low, t[3], t[0]), 4, 1),
        jnp.where(low, t[1], t[3]),
        pltpu.roll(jnp.where(low, t[4], t[1]), 4, 1),
        jnp.where(low, t[2], t[4]),
    ]
    return [u.reshape(N, 128) for u in units]


def units_to(ref, units):
    a, b, c, d, e = [u.reshape(64, 8, 128) for u in units]
    low = iota((64, 8, 128), 1) < 4
    turned_b, turned_d = pltpu.roll(b, 4, 1), pltpu.roll(d, 4, 1)
    tiles = [
        jnp.where(low, a, turned_b),
        jnp.where(low, c, turned_d),
        jnp.where(low, e, a),
        jnp.where(low, turned_b, c),
        jnp.where(low, turned_d, e),
    ]
    tiles = jnp.concatenate(tiles, axis=1).astype(BF)
    for i in range(64):
        ref[PLACE[i]] = tiles[i]


def transport(codes, at, f):
    taps = []
    for i in range(4):
        part = codes[128 * i : 128 * i + 128]
        rel = part[:, at : at + 1]
        pieces = [[part[:, at + j + k : at + j + 1 + k] for k in range(4)] for j in (1, 5)]
        moved = []
        for tile, first, count in ((0, 0, 128), (-1, 0, 16), (1, 112, 16)):
            rows = slice(first, first + count)
            row = iota((count, 128), 0) + first
            lag = (iota((count, 128), 1) + 128 * tile - (row & -4)).astype(F32) - rel[rows]
            band = []
            for piece in pieces:
                weight = jnp.zeros((count, 128), F32)
                for k in range(4):
                    weight = jnp.where(lag == k, piece[k][rows], weight)
                band.append(weight.astype(BF))
            j = (i + tile) % 4
            source = f[128 * j : 128 * j + 128]
            moved.append(dot(jnp.concatenate(band, axis=1), jnp.concatenate([source, source], axis=0)))
        mid, down, up = moved
        taps += [mid[:16] + down, mid[16:112], mid[112:] + up]
    return jnp.concatenate(taps, axis=0).astype(BF)


def transport_kernel(got_ref, deriv_ref, out0_ref, out1_ref, out2_ref, out3_ref, warped_ref, pieces):
    me = lax.axis_index("pencil")
    own, partner, other, image, codes = planes_of(got_ref)
    near = jnp.concatenate([own, partner], axis=1).astype(BF)
    other = other.astype(BF)
    for section in range(2):
        near = transport(codes, 16 * section, near)
        other = transport(codes, 32 + 16 * section, other)
    warped = near[:, :128]
    residual = image - warped.astype(F32)
    image = image.astype(BF)
    sign = jnp.where((me & 2) == 0, 0.5, -0.5).astype(F32)
    slope_z = (near[:, 128:].astype(F32) - other.astype(F32)) * sign
    warped_ref[...] = warped
    pieces[0] = (residual * dot(deriv_ref[...], warped)).astype(BF)
    pieces[1, 0:256] = warped[0:256]
    pieces[1, 256:512] = image[0:256]
    pieces[2] = (residual * slope_z).astype(BF)
    pieces[3, 0:256] = warped[256:512]
    pieces[3, 256:512] = image[256:512]
    for s, ref in enumerate((out0_ref, out1_ref, out2_ref, out3_ref)):
        ref[...] = pieces[quarter_of(me) ^ s]


def smooth_kernel(p0_ref, p1_ref, p2_ref, p3_ref, warped_ref, deriv_ref, table_ref, flip_ref, out_ref, plane):
    role = quarter_of(lax.axis_index("pencil"))
    for s, ref in enumerate((p0_ref, p1_ref, p2_ref, p3_ref)):
        plane[:, pl.ds(pl.multiple_of((role ^ s) * 128, 128), 128)] = ref[...]

    @pl.when((role & 1) == 1)
    def _():
        half = plane[0:256]
        slope_y = -dot(half, deriv_ref[...])
        force = ((plane[256:512].astype(F32) - half.astype(F32)) * slope_y).astype(BF)
        at = (role >> 1) * 256
        plane[pl.ds(pl.multiple_of(at, 256), 256)] = force
        plane[pl.ds(pl.multiple_of(256 - at, 256), 256)] = jnp.zeros((256, N), BF)

    spec = dot(plane[...], flip_ref[...]).astype(BF)
    wave_x, scale_x = mode_waves((N, 1), 0)
    wave_y, scale_y = mode_waves((1, N), 1)
    gain = (scale_x * scale_y * (FORCE_GAIN / (N * N))) / (1.0 + H1_WEIGHT * (wave_x * wave_x + wave_y * wave_y))
    bent = (dot(table_ref[...], spec) * gain).astype(BF)
    back = dot(flip_ref[...], bent).astype(BF)
    smooth = dot(back, table_ref[...])
    units = [smooth[:, 128 * s : 128 * s + 128] for s in range(4)]
    units_to(out_ref, units + [warped_ref[...].astype(F32)])


def finish_kernel(home_ref, pick_ref, velocity_ref, out_warped_ref, out_ref, velocity, result, warped, sem):
    loads = fetch([velocity_ref.at[c] for c in range(3)], [velocity.at[c] for c in range(3)], sem)
    pick = pick_ref[...]
    units = units_of(home_ref)
    rows = jnp.concatenate(units[:4], axis=1).astype(BF)
    turned = dot(pick, units[4].astype(BF))
    for r in range(4):
        warped[:, :, 128 * r : 128 * r + 128] = turned[128 * r : 128 * r + 128].reshape(4, 32, 128).astype(BF)
    stores = [pltpu.make_async_copy(warped, out_warped_ref, sem.at[3])]
    stores[0].start()
    for c in range(3):
        which = pick[128 * c : 128 * c + 128]
        if c == 1:
            which = which + pick[384:512]
        part = dot(which, rows).reshape(4, 32, N)
        loads[c].wait()
        result[c] = velocity[c] + part
        store = pltpu.make_async_copy(result.at[c], out_ref.at[c], sem.at[4 + c])
        store.start()
        stores.append(store)
    for store in stores:
        store.wait()


ANY = pl.BlockSpec(memory_space=pltpu.HBM)
VMEM = pl.BlockSpec(memory_space=pltpu.VMEM)


def call(kernel, outs, in_specs, out_specs, scratch, grant=48 << 20):
    return pl.pallas_call(
        kernel,
        out_shape=outs,
        in_specs=in_specs,
        out_specs=out_specs,
        scratch_shapes=scratch,
        compiler_params=pltpu.CompilerParams(vmem_limit_bytes=grant),
    )


def swap(chunks, rows, order):
    chunks_of = chunks.reshape(-1, rows, 128)
    chunks_of = lax.all_to_all(chunks_of, "pencil", 0, 0, axis_index_groups=[order], tiled=True)
    return chunks_of.reshape(chunks.shape)


def local(template, reference_image, velocity, dep_owner, dep_offset, dep_weight):
    shape = jax.ShapeDtypeStruct
    piece = shape((N, 128), BF)
    vm = pltpu.VMEM

    pick = bf(pack_rows())
    inputs = (dep_owner, dep_offset, dep_weight, template, reference_image, pick)
    pack = call(
        pack_kernel,
        shape((32, 72, 128), BF),
        [ANY] * 6,
        VMEM,
        [vm(a.shape, a.dtype) for a in inputs] + [pltpu.SemaphoreType.DMA((6,))],
        65000000,
    )(*inputs)
    got = swap(pack, 2, ORDERS[0])

    deriv = bf(derivative_matrix())
    *parts, warped = call(
        transport_kernel,
        [piece] * 5,
        [VMEM] * 2,
        [VMEM] * 5,
        [vm((4, N, 128), BF)],
    )(got, deriv)
    for s in (1, 2, 3):
        parts[s] = lax.ppermute(parts[s], "pencil", [(i ^ PARTNER[s], i) for i in range(128)])

    table = basis(np.arange(N))
    send = call(
        smooth_kernel,
        shape((64, 40, 128), BF),
        [VMEM] * 8,
        VMEM,
        [vm((N, N), BF)],
    )(*parts, warped, deriv, bf(table), bf(table.T))
    home = swap(send, 4, ORDERS[1])

    return call(
        finish_kernel,
        [shape((4, 32, N), BF), shape((3, 4, 32, N), F32)],
        [VMEM, VMEM, ANY],
        [ANY, ANY],
        [vm((3, 4, 32, N), F32), vm((3, 4, 32, N), F32), vm((4, 32, N), BF), pltpu.SemaphoreType.DMA((7,))],
    )(home, bf(unpack_rows()), velocity)


def solution(mesh):
    in_specs = (
        P("pencil", "start", None),
        P("pencil", "start", None),
        P("start", "pencil", None, None),
        P("start", "pencil"),
        P("start", "pencil"),
        P("start", "pencil"),
    )
    out_specs = (P("pencil", "start", None), P("start", "pencil", None, None))
    return jax.shard_map(local, mesh=mesh, in_specs=in_specs, out_specs=out_specs, check_vma=False)
```

```python
import math

import jax
import jax.numpy as jnp
import numpy as np
from jax import lax
from jax.experimental import pallas as pl
from jax.experimental.pallas import tpu as pltpu
from jax.sharding import PartitionSpec as P

Q = 16
N = 512
H1_WEIGHT = 64.0
FORCE_GAIN = 32.0
BF = jnp.bfloat16
F32 = jnp.float32
NN = ((1,), (0,))
NT = ((1,), (1,))


def wave_numbers():
    k = np.arange(N)
    signed = np.where(k < N // 2, k, k - N)
    signed = np.where(k == N // 2, 0, signed)
    return signed * (2.0 * math.pi / N)


def derivative_matrix():
    k = np.arange(N)
    lag = np.arange(N)
    row = (np.sin(2.0 * math.pi * ((k[:, None] * lag[None, :]) % N) / N) * wave_numbers()[:, None]).sum(0) / N
    return row[(lag[None, :] - lag[:, None]) % N]


def modes():
    return np.concatenate([np.arange(N // 2 + 1), np.arange(1, N // 2)])


def basis(points):
    angle = 2.0 * math.pi * ((modes()[:, None] * points[None, :]) % N) / N
    is_cos = (np.arange(N) <= N // 2)[:, None]
    return np.where(is_cos, np.cos(angle), np.sin(angle))


def pack_rows():
    pick = np.zeros((32, 24, 320), np.float32)
    for z in range(32):
        other = (z + (1 if z % 2 else -1)) % 32
        for x in range(4):
            pick[z, x, x * 32 + z] = 1
            pick[z, 4 + x, x * 32 + (z ^ 1)] = 1
            pick[z, 8 + x, x * 32 + other] = 1
            pick[z, 12 + x, 128 + x * 32 + z] = 1
        pick[z, 16, 256 + z * 2] = 1
        pick[z, 17, 257 + z * 2] = 1
    return pick.reshape(768, 320)


def unpack_rows():
    r = np.arange(N)
    role, x, z = r // 128, (r // 32) % 4, r % 32
    device = (z // 2) * 8 + (role // 2) * 4 + (z % 2) * 2 + role % 2
    pick = np.zeros((N, N), np.float32)
    pick[r, (np.array(PLACE)[device // 2] * 2 + device % 2) * 4 + x] = 1
    return pick


QUADS = [int(i) for i in np.random.RandomState(1).permutation(32)]
PAIRS = [int(i) for i in np.random.RandomState(24).permutation(64)]
ORDERS = [[4 * i + j for i in QUADS for j in range(4)], [2 * i + j for i in PAIRS for j in (0, 1)]]
QUAD_PLACE = [QUADS.index(i) for i in range(32)]
PLACE = [PAIRS.index(i) for i in range(64)]

PARTNER = (0, 1, 4, 5)


def quarter_of(device):
    return ((device >> 1) & 2) + (device & 1)


def bf(x):
    return jnp.asarray(np.asarray(x, np.float32), BF)


def dot(a, b, dims=NN):
    return lax.dot_general(a, b, (dims, ((), ())), preferred_element_type=F32)


def iota(shape, axis):
    return lax.broadcasted_iota(jnp.int32, shape, axis)


def cubic(level):
    t = (level + 0.5) / Q
    return [
        -t * (t - 1.0) * (t - 2.0) / 6.0,
        (t + 1.0) * (t - 1.0) * (t - 2.0) / 2.0,
        -(t + 1.0) * t * (t - 2.0) / 2.0,
        (t + 1.0) * t * (t - 1.0) / 6.0,
    ]


def mode_waves(shape, axis):
    i = iota(shape, axis)
    k = jnp.where(i < N // 2, i, i - N // 2)
    wave = k.astype(F32) * (2.0 * math.pi / N)
    return wave, jnp.where(k == 0, 1.0, 2.0)


def fetch(refs, scratch, sem):
    copies = [pltpu.make_async_copy(r, v, sem.at[i]) for i, (r, v) in enumerate(zip(refs, scratch))]
    for copy in copies:
        copy.start()
    return copies


def pack_kernel(owner_ref, offset_ref, weight_ref, template_ref, image_ref, pick_ref, out_ref, owner, offset, weight, template, image, pick, sem):
    copies = fetch(
        (owner_ref, offset_ref, weight_ref, template_ref, image_ref, pick_ref),
        (owner, offset, weight, template, image, pick),
        sem,
    )
    me = lax.axis_index("pencil")
    for copy in copies[:3]:
        copy.wait()
    move = ((owner[...] - me + 130) & 127) - 2
    rel = (move * 4 + (offset[...] >> 6)).astype(F32)
    level = weight[...].astype(F32)
    taps = cubic(level)
    items = [rel]
    for tap in taps:
        items.append(tap.astype(BF).astype(F32))
    for tap, high in zip(taps, items[1:5]):
        items.append(tap - high)
    row = iota((32, 256), 0)
    value = jnp.zeros((32, 256), F32)
    for section in range(2):
        for i, item in enumerate(items):
            value = jnp.where(row == 16 * section + i, item[section : section + 1], value)
    blank = jnp.zeros((32, 256), F32)
    codes = jnp.concatenate(
        [jnp.concatenate([value if i == j else blank for j in range(4)], axis=1) for i in range(4)], axis=0
    ).astype(BF)
    row, col = iota((256, 256), 0), iota((256, 256), 1)
    q, z = row >> 6, (row >> 1) & 31
    other = (z + 2 * (z & 1) - 1) & 31
    hot = [
        jnp.where(col == (2 * (row & 1) + x) * 64 + (plane >> 1) * 4 + q, 1.0, 0.0)
        for x in range(2)
        for plane in (z, other)
    ]
    codes = dot(jnp.concatenate(hot, axis=1).astype(BF), codes, NT).astype(BF)
    codes = jnp.concatenate([codes[64 * i : 64 * i + 64] for i in range(4)], axis=1)
    for copy in copies[3:]:
        copy.wait()
    stack = jnp.concatenate([template[...].reshape(128, N), image[...].reshape(128, N), codes], axis=0)
    rows = dot(pick[...], stack)
    at = iota((16, 8, 128), 1)
    for half in range(2):
        chunks = []
        for j in range(4):
            q = 2 * half + (j & 1)
            part = rows[:, 128 * q : 128 * q + 128].reshape(16, 2, 3, 8, 128)[:, j >> 1]
            part = [part[:, i] for i in range(3)]
            chunks.append([pltpu.roll(v, 2 * j, 1) for v in part] if j else part)
        (a0, b0, c0), (a1, b1, c1), (a2, b2, c2), (a3, b3, c3) = chunks
        tiles = [
            a0,
            b0,
            jnp.where(at < 2, c0, a1),
            jnp.where(at < 2, a1, b1),
            jnp.where(at < 2, b1, jnp.where(at < 4, c1, a2)),
            jnp.where(at < 4, a2, b2),
            jnp.where(at < 4, b2, jnp.where(at < 6, c2, a3)),
            jnp.where(at < 6, a3, b3),
            jnp.where(at < 6, b3, c3),
        ]
        tiles = jnp.concatenate(tiles, axis=1).astype(BF)
        for z in range(16):
            out_ref[QUAD_PLACE[2 * z + half]] = tiles[z]


def planes_of(ref):
    t = [ref[:, 8 * i : 8 * i + 8, :].astype(F32) for i in range(9)]
    t = [jnp.concatenate([v[i : i + 1] for i in QUAD_PLACE], axis=0) for v in t]
    at = iota((32, 8, 128), 1)
    low = at < 4

    def turn(v, by):
        return pltpu.roll(v, by, 1)

    def join(first, second):
        return jnp.stack([first, second], axis=1).reshape(N, 128)

    units = []
    for i in range(2):
        v0 = t[i]
        v1 = jnp.where(at < 2, t[3 + i], t[2 + i])
        v2 = jnp.where(low, t[5 + i], t[4 + i])
        v3 = jnp.where(at < 6, t[7 + i], t[6 + i])
        units.append(join(jnp.where(low, v0, turn(v1, 2)), jnp.where(low, turn(v2, 4), turn(v3, 6))))
        units.append(join(jnp.where(low, turn(v0, 4), turn(v1, 6)), jnp.where(low, v2, turn(v3, 2))))
    codes = []
    for v in (jnp.where(low, t[2], turn(t[4], 2)), jnp.where(low, turn(t[6], 4), turn(t[8], 6))):
        v = jnp.where((at & 3) == 0, v, jnp.where((at & 3) == 3, turn(v, 2), turn(v, 1)))
        codes.append(jnp.where((at & 1) == 1, pltpu.roll(v, 64, 2), v))
    return units + [join(*codes)]


def units_of(ref):
    t = [ref[:, 8 * i : 8 * i + 8, :].astype(F32) for i in range(5)]
    low = iota((64, 8, 128), 1) < 4
    units = [
        jnp.where(low, t[0], t[2]),
        pltpu.roll(jnp.where(low, t[3], t[0]), 4, 1),
        jnp.where(low, t[1], t[3]),
        pltpu.roll(jnp.where(low, t[4], t[1]), 4, 1),
        jnp.where(low, t[2], t[4]),
    ]
    return [u.reshape(N, 128) for u in units]


def units_to(ref, units):
    a, b, c, d, e = [u.reshape(64, 8, 128) for u in units]
    low = iota((64, 8, 128), 1) < 4
    turned_b, turned_d = pltpu.roll(b, 4, 1), pltpu.roll(d, 4, 1)
    tiles = [
        jnp.where(low, a, turned_b),
        jnp.where(low, c, turned_d),
        jnp.where(low, e, a),
        jnp.where(low, turned_b, c),
        jnp.where(low, turned_d, e),
    ]
    tiles = jnp.concatenate(tiles, axis=1).astype(BF)
    for i in range(64):
        ref[PLACE[i]] = tiles[i]


def transport(codes, at, f):
    taps = []
    weights = codes + pltpu.roll(codes, 124, 1)
    for i in range(4):
        part = codes[128 * i : 128 * i + 128]
        whole = weights[128 * i : 128 * i + 128]
        rel = part[:, at : at + 1]
        levels = [whole[:, at + 1 + k : at + 2 + k] for k in range(4)]
        moved = []
        for tile, first, count in ((0, 0, 128), (-1, 0, 16), (1, 112, 16)):
            rows = slice(first, first + count)
            row = iota((count, 128), 0) + first
            lag = (iota((count, 128), 1) + 128 * tile - (row & -4)).astype(F32) - rel[rows]
            weight = jnp.zeros((count, 128), F32)
            for k in range(4):
                weight = jnp.where(lag == k, levels[k][rows], weight)
            high = weight.astype(BF)
            band = [high, (weight - high.astype(F32)).astype(BF)]
            j = (i + tile) % 4
            source = f[128 * j : 128 * j + 128]
            moved.append(dot(jnp.concatenate(band, axis=1), jnp.concatenate([source, source], axis=0)))
        mid, down, up = moved
        taps += [mid[:16] + down, mid[16:112], mid[112:] + up]
    return jnp.concatenate(taps, axis=0).astype(BF)


def transport_kernel(got_ref, deriv_ref, out0_ref, out1_ref, out2_ref, out3_ref, warped_ref, pieces):
    me = lax.axis_index("pencil")
    own, partner, other, image, codes = planes_of(got_ref)
    near = jnp.concatenate([own, partner], axis=1).astype(BF)
    other = other.astype(BF)
    for section in range(2):
        near = transport(codes, 16 * section, near)
        other = transport(codes, 32 + 16 * section, other)
    warped = near[:, :128]
    residual = image - warped.astype(F32)
    image = image.astype(BF)
    sign = jnp.where((me & 2) == 0, 0.5, -0.5).astype(F32)
    slope_z = (near[:, 128:].astype(F32) - other.astype(F32)) * sign
    warped_ref[...] = warped
    pieces[0] = (residual * dot(deriv_ref[...], warped)).astype(BF)
    pieces[1, 0:256] = warped[0:256]
    pieces[1, 256:512] = image[0:256]
    pieces[2] = (residual * slope_z).astype(BF)
    pieces[3, 0:256] = warped[256:512]
    pieces[3, 256:512] = image[256:512]
    for s, ref in enumerate((out0_ref, out1_ref, out2_ref, out3_ref)):
        ref[...] = pieces[quarter_of(me) ^ s]


def smooth_kernel(p0_ref, p1_ref, p2_ref, p3_ref, warped_ref, deriv_ref, table_ref, flip_ref, out_ref, plane):
    role = quarter_of(lax.axis_index("pencil"))
    for s, ref in enumerate((p0_ref, p1_ref, p2_ref, p3_ref)):
        plane[:, pl.ds(pl.multiple_of((role ^ s) * 128, 128), 128)] = ref[...]

    @pl.when((role & 1) == 1)
    def _():
        half = plane[0:256]
        slope_y = -dot(half, deriv_ref[...])
        force = ((plane[256:512].astype(F32) - half.astype(F32)) * slope_y).astype(BF)
        at = (role >> 1) * 256
        plane[pl.ds(pl.multiple_of(at, 256), 256)] = force
        plane[pl.ds(pl.multiple_of(256 - at, 256), 256)] = jnp.zeros((256, N), BF)

    spec = dot(plane[...], flip_ref[...]).astype(BF)
    wave_x, scale_x = mode_waves((N, 1), 0)
    wave_y, scale_y = mode_waves((1, N), 1)
    gain = (scale_x * scale_y * (FORCE_GAIN / (N * N))) / (1.0 + H1_WEIGHT * (wave_x * wave_x + wave_y * wave_y))
    bent = (dot(table_ref[...], spec) * gain).astype(BF)
    back = dot(flip_ref[...], bent).astype(BF)
    smooth = dot(back, table_ref[...])
    units = [smooth[:, 128 * s : 128 * s + 128] for s in range(4)]
    units_to(out_ref, units + [warped_ref[...].astype(F32)])


def finish_kernel(home_ref, pick_ref, velocity_ref, out_warped_ref, out_ref, velocity, result, warped, sem):
    loads = fetch([velocity_ref.at[c] for c in range(3)], [velocity.at[c] for c in range(3)], sem)
    pick = pick_ref[...]
    units = units_of(home_ref)
    rows = jnp.concatenate(units[:4], axis=1).astype(BF)
    turned = dot(pick, units[4].astype(BF))
    for r in range(4):
        warped[:, :, 128 * r : 128 * r + 128] = turned[128 * r : 128 * r + 128].reshape(4, 32, 128).astype(BF)
    stores = [pltpu.make_async_copy(warped, out_warped_ref, sem.at[3])]
    stores[0].start()
    for c in range(3):
        which = pick[128 * c : 128 * c + 128]
        if c == 1:
            which = which + pick[384:512]
        part = dot(which, rows).reshape(4, 32, N)
        loads[c].wait()
        result[c] = velocity[c] + part
        store = pltpu.make_async_copy(result.at[c], out_ref.at[c], sem.at[4 + c])
        store.start()
        stores.append(store)
    for store in stores:
        store.wait()


ANY = pl.BlockSpec(memory_space=pltpu.HBM)
VMEM = pl.BlockSpec(memory_space=pltpu.VMEM)


def call(kernel, outs, in_specs, out_specs, scratch, grant=48 << 20):
    return pl.pallas_call(
        kernel,
        out_shape=outs,
        in_specs=in_specs,
        out_specs=out_specs,
        scratch_shapes=scratch,
        compiler_params=pltpu.CompilerParams(vmem_limit_bytes=grant),
    )


def swap(chunks, rows, order):
    chunks_of = chunks.reshape(-1, rows, 128)
    chunks_of = lax.all_to_all(chunks_of, "pencil", 0, 0, axis_index_groups=[order], tiled=True)
    return chunks_of.reshape(chunks.shape)


def local(template, reference_image, velocity, dep_owner, dep_offset, dep_weight):
    shape = jax.ShapeDtypeStruct
    piece = shape((N, 128), BF)
    vm = pltpu.VMEM

    pick = bf(pack_rows())
    inputs = (dep_owner, dep_offset, dep_weight, template, reference_image, pick)
    pack = call(
        pack_kernel,
        shape((32, 72, 128), BF),
        [ANY] * 6,
        VMEM,
        [vm(a.shape, a.dtype) for a in inputs] + [pltpu.SemaphoreType.DMA((6,))],
        65000000,
    )(*inputs)
    got = swap(pack, 2, ORDERS[0])

    deriv = bf(derivative_matrix())
    *parts, warped = call(
        transport_kernel,
        [piece] * 5,
        [VMEM] * 2,
        [VMEM] * 5,
        [vm((4, N, 128), BF)],
    )(got, deriv)
    for s in (1, 2, 3):
        parts[s] = lax.ppermute(parts[s], "pencil", [(i ^ PARTNER[s], i) for i in range(128)])

    table = basis(np.arange(N))
    send = call(
        smooth_kernel,
        shape((64, 40, 128), BF),
        [VMEM] * 8,
        VMEM,
        [vm((N, N), BF)],
    )(*parts, warped, deriv, bf(table), bf(table.T))
    home = swap(send, 4, ORDERS[1])

    return call(
        finish_kernel,
        [shape((4, 32, N), BF), shape((3, 4, 32, N), F32)],
        [VMEM, VMEM, ANY],
        [ANY, ANY],
        [vm((3, 4, 32, N), F32), vm((3, 4, 32, N), F32), vm((4, 32, N), BF), pltpu.SemaphoreType.DMA((7,))],
    )(home, bf(unpack_rows()), velocity)


def solution(mesh):
    in_specs = (
        P("pencil", "start", None),
        P("pencil", "start", None),
        P("start", "pencil", None, None),
        P("start", "pencil"),
        P("start", "pencil"),
        P("start", "pencil"),
    )
    out_specs = (P("pencil", "start", None), P("start", "pencil", None, None))
    return jax.shard_map(local, mesh=mesh, in_specs=in_specs, out_specs=out_specs, check_vma=False)
```
